32 devices in a mesh: row: 4 (over y, core), col: 8 (over z, x).
Axes of the slice: x: 2, y: 2, z: 4, core: 2. Of those that a mesh axis runs over, the one named last changes fastest.
Arguments:
- matrix: float32 [16384, 16384], P('row', 'col'), as said below
Outputs:
- updated: float32 [16384, 16384], P('row', 'col')
- reflectors: float32 [1, 16384, 256], P(None, ('row', 'col'))
- products: float32 [1, 16384, 256], P(None, ('row', 'col'))
Inputs may be any that keep to these rules, and one draw needn't show every extreme that they name: `matrix`: symmetric.
All inputs are finite; a program needn't handle non-finite values.
Results may differ from the reference program's by a relative error of at most 0.0003.
Values sent between devices are 32-bit elements; how exact they have to be, the bound alone decides.
A program may use at most 192 MiB of HBM per device.

```python
import math
import jax
import jax.numpy as jnp
from jax import lax

ORDER = 16384
NB = 256
PANELS = 1


def draw_matrix(key, part):
    noise_key = jax.random.fold_in(key, 11)
    block_key = jax.random.fold_in(key, 23)
    noise = jax.random.normal(noise_key, (ORDER, ORDER), jnp.float32)
    sym_part = (noise + noise.T) * 0.7071
    diag_scale = 2.0 * math.sqrt(ORDER)
    spread = 0.35 * diag_scale / math.sqrt(NB)
    blocks = jax.random.normal(block_key, (2, NB, NB), jnp.float32) * spread
    blocks = blocks + diag_scale * jnp.eye(NB, dtype=jnp.float32)[None, :, :]
    planted = jnp.zeros((ORDER, ORDER), jnp.float32)
    planted = planted.at[NB:2 * NB, 0:NB].set(blocks[0])
    planted = planted.at[2 * NB:3 * NB, NB:2 * NB].set(blocks[1])
    result = sym_part + planted + planted.T
    return result


def setup_inputs(seed: int = 0) -> dict:
    key_of = jax.random.split(jax.random.key(seed), 2)
    matrix = draw_matrix(jax.random.fold_in(key_of[1], 71), 0)
    return {"matrix": matrix}


def matmul(left, right):
    return jnp.dot(left.astype(jnp.float32), right.astype(jnp.float32), precision=lax.Precision.HIGHEST, preferred_element_type=jnp.float32)

def lu_signed(square):
    order_n = square.shape[0]
    all_ids = jnp.arange(order_n)

    def lu_step(pivot_idx, state):
        work_mat, sign_vec = state
        column = work_mat[:, pivot_idx]
        raw_pivot = column[pivot_idx]
        sign_now = jnp.where(raw_pivot >= 0, 1.0, -1.0)
        pivot_val = raw_pivot + sign_now
        lower_col = jnp.where(all_ids > pivot_idx, column / pivot_val, 0.0)
        upper_row = jnp.where(all_ids > pivot_idx, work_mat[pivot_idx, :], 0.0)
        work_mat = work_mat - lower_col[:, None] * upper_row[None, :]
        kept = jnp.where(all_ids > pivot_idx, lower_col, jnp.where(all_ids == pivot_idx, pivot_val, column))
        work_mat = work_mat.at[:, pivot_idx].set(kept)
        sign_vec = sign_vec.at[pivot_idx].set(sign_now)
        return (work_mat, sign_vec)
    packed, sign_vec = lax.fori_loop(0, order_n, lu_step, (square, jnp.zeros((order_n,), square.dtype)))
    unit_lower = jnp.tril(packed, -1) + jnp.eye(order_n, dtype=square.dtype)
    return (unit_lower, jnp.triu(packed), sign_vec)

def reference(matrix):
    row_ids = jnp.arange(matrix.shape[0])
    current = matrix
    all_refl = []
    all_prod = []
    for panel_idx in range(PANELS):
        col_start = panel_idx * NB
        row_start = col_start + NB
        panel_cols = jnp.where((row_ids >= row_start)[:, None], current[:, col_start:col_start + NB], 0.0)
        gram_sum = matmul(panel_cols.T, panel_cols)
        chol_low = jnp.linalg.cholesky(gram_sum)
        q_basis = jax.scipy.linalg.solve_triangular(chol_low, panel_cols.T, lower=True).T
        top_block = q_basis[row_start:row_start + NB]
        unit_lower, upper_tri, sign_diag = lu_signed(top_block)
        solved = jax.scipy.linalg.solve_triangular(upper_tri.T, q_basis.T, lower=True).T
        rel_pos = row_ids - row_start
        in_top = (rel_pos >= 0) & (rel_pos < NB)
        lower_rows = jnp.take(unit_lower, jnp.clip(rel_pos, 0, NB - 1), axis=0)
        refl = jnp.where(in_top[:, None], lower_rows, jnp.where((rel_pos < 0)[:, None], 0.0, solved))
        scaled = upper_tri * sign_diag[None, :]
        t_factor = jax.scipy.linalg.solve_triangular(unit_lower, scaled.T, lower=True, unit_diagonal=True).T
        x_rows = matmul(current, matmul(refl, t_factor))
        inner_prod = matmul(refl.T, x_rows)
        w_rows = x_rows - 0.5 * matmul(refl, matmul(t_factor.T, inner_prod))
        current = current - matmul(refl, w_rows.T) - matmul(w_rows, refl.T)
        all_refl.append(refl)
        all_prod.append(w_rows)
    return (current, jnp.stack(all_refl), jnp.stack(all_prod))
```

```python
import functools

import jax
import jax.numpy as jnp
from jax import lax
from jax.experimental import pallas as pl
from jax.experimental.pallas import tpu as pltpu
from jax.sharding import PartitionSpec as P

NB = 256
STRIP = 16
LANES = 128
MESH = pl.DeviceIdType.MESH
F32 = jnp.float32
BF16 = jnp.bfloat16


def exact(left, right, dims=((1,), (0,))):
    return lax.dot_general(
        left, right, (dims, ((), ())),
        precision=lax.Precision.HIGHEST, preferred_element_type=F32,
    )


def split3(left, right, dims=((1,), (0,))):
    return lax.dot_general(
        left, right, (dims, ((), ())),
        precision=lax.Precision.HIGH, preferred_element_type=F32,
    )


def halves(value):
    high = value.astype(BF16)
    return high, (value - high.astype(F32)).astype(BF16)


def dot(left, right, dims=((1,), (0,))):
    return lax.dot_general(left, right, (dims, ((), ())), preferred_element_type=F32)


def dot3(left, right, dims=((1,), (0,))):
    (lh, ll), (rh, rl) = left, right
    return dot(lh, rh, dims) + (dot(lh, rl, dims) + dot(ll, rh, dims))


def wide(part, n):
    return jnp.concatenate([part] * (n // part.shape[1]), axis=1)


FACTOR_SCRATCH = 7


def factor_scratch(n):
    return [pltpu.VMEM((n, n), F32)] * FACTOR_SCRATCH + [pltpu.VMEM((n, LANES), F32)]


def factor_body(gram, top, rinvt_out, linv_out, shape_out, low_out, tft_out,
                wg, wt, fg, ft, lead, bd, bl, sg):
    n = gram.shape[0]
    strip = STRIP
    lanes = lax.broadcasted_iota(jnp.int32, (strip, n), 1)
    subs = lax.broadcasted_iota(jnp.int32, (strip, n), 0)
    lane = lax.broadcasted_iota(jnp.int32, (1, n), 1)
    subs1 = lax.broadcasted_iota(jnp.int32, (strip, LANES), 0)
    full = lax.broadcasted_iota(jnp.int32, (n, n), 1)
    wg[...] = gram
    wt[...] = top
    lead[...] = jnp.zeros_like(lead)

    def one(s, carry):
        at = pl.ds(pl.multiple_of(s * strip, strip), strip)
        g, t = wg[at, :], wt[at, :]
        keep = n - s * strip
        gc = [jnp.broadcast_to(g[:, j : j + 1], (strip, LANES)) for j in range(strip)]
        tc = [jnp.broadcast_to(t[:, j : j + 1], (strip, LANES)) for j in range(strip)]
        gf, tf, ld = g, t, jnp.where(lanes == subs, 1.0, 0.0)
        signs = jnp.zeros((strip, LANES), F32)
        for k in range(strip):
            gcol, gp = gc[k], gc[k][k : k + 1]
            root = 1.0 / jnp.sqrt(gp)
            ginv = root * root
            tcol, tp = tc[k], tc[k][k : k + 1]
            sign = jnp.where(tp >= 0, 1.0, -1.0)
            add = sign * root
            tinv = 1.0 / (tp + add * gp)
            grow = g[k : k + 1]
            trow = t[k : k + 1] + jnp.where((lane >= k) & (lane < keep), grow, 0.0) * wide(add, n)
            gf = jnp.where(subs == k, grow, gf)
            tf = jnp.where(subs == k, trow, tf)
            signs = jnp.where(subs1 == k, sign, signs)
            gscaled = jnp.where(lane == k, wide(ginv, n), grow * wide(ginv, n))
            tscaled = jnp.where(lane == k, wide(tinv, n), trow * wide(tinv, n))
            ld = jnp.where((lanes == k) & (subs > k), wide(tcol * tinv, n), ld)
            for j in range(k + 1, strip):
                grj = gc[j][k : k + 1]
                trj = (tc[j][k : k + 1] + add * grj) * tinv
                grj = grj * ginv
                gc[j] = jnp.where(subs1 == k, grj, gc[j] - gcol * grj)
                tc[j] = jnp.where(subs1 == k, trj, tc[j] - tcol * trj)
            g = jnp.where(subs == k, gscaled, jnp.where(lanes == k, 0.0, g) - wide(gcol, n) * gscaled)
            t = jnp.where(subs == k, tscaled, jnp.where(lanes == k, 0.0, t) - wide(tcol, n) * tscaled)
        back = s * strip
        fg[at, :] = pltpu.roll(gf, back, 1)
        ft[at, :] = pltpu.roll(tf, back, 1)
        bl[at, :] = pltpu.roll(ld, back, 1)
        bd[at, :] = pltpu.roll(jnp.where(lanes < strip, t, 0.0), back, 1)
        sg[at, :] = signs
        gw, tw = wg[...], wt[...]
        step = n - strip
        lead[...] = pltpu.roll(jnp.where(full < strip, tw, lead[...]), step, 1)
        gn = jnp.where(full < strip, 0.0, gw) - exact(gw[:, :strip], g)
        tn = jnp.where(full < strip, 0.0, tw) - exact(tw[:, :strip], t)
        wg[...] = pltpu.roll(gn, step, 1)
        wt[...] = pltpu.roll(tn, step, 1)
        wg[at, :] = pltpu.roll(g, step, 1)
        wt[at, :] = pltpu.roll(t, step, 1)
        return carry

    lax.fori_loop(0, n // strip, one, 0)
    rows = lax.broadcasted_iota(jnp.int32, (n, n), 0)
    cols = lax.broadcasted_iota(jnp.int32, (n, n), 1)
    eye = jnp.where(rows == cols, 1.0, 0.0)
    diag = jnp.sum(fg[...] * eye, axis=1, keepdims=True)
    rinvt = jnp.where(rows > cols, fg[...], eye) * (1.0 / jnp.sqrt(diag)) * wide(sg[...], n)
    linv = jnp.where(rows > cols, ft[...], eye)
    upper = jnp.where(rows <= cols, ft[...], 0.0)
    rinvt_out[...] = rinvt
    linv_out[...] = linv
    tft_out[...] = exact(linv, exact(rinvt, upper, ((1,), (1,))))
    low = exact(exact(jnp.where(rows >= cols - cols % strip, lead[...], 0.0), bd[...]), bl[...])
    low = jnp.where(rows > cols, low, eye)
    low_out[...] = low
    shape_out[...] = jnp.where(rows <= cols, exact(wt[...], low), 0.0)


def factor_kernel(gram_ref, top_ref, *refs):
    factor_body(gram_ref[...], top_ref[...], *refs)


def factor(gram, top):
    n = gram.shape[0]
    square = jax.ShapeDtypeStruct((n, n), F32)
    return pl.pallas_call(
        factor_kernel,
        out_shape=[square] * 5,
        in_specs=[pl.BlockSpec(memory_space=pltpu.VMEM)] * 2,
        out_specs=[pl.BlockSpec(memory_space=pltpu.VMEM)] * 5,
        scratch_shapes=factor_scratch(n),
        compiler_params=pltpu.CompilerParams(vmem_limit_bytes=16 * 1024 * 1024),
        cost_estimate=pl.CostEstimate(flops=2_000_000_000, bytes_accessed=2_000_000, transcendentals=0),
        name="factor",
    )(gram, top)


def greet(partners):
    barrier = pltpu.get_barrier_semaphore()
    for device in partners:
        pl.semaphore_signal(barrier, inc=1, device_id=device, device_id_type=MESH)
    pl.semaphore_wait(barrier, len(partners))


def cross(r, c, n_row, n_col):
    return ([(lax.rem(r + k, n_row), c) for k in range(1, n_row)]
            + [(r, lax.rem(c + k, n_col)) for k in range(1, n_col)])


def trees(x, z, wide_x, deep_z):
    first = [
        ((z == 0) & (x < wide_x - 1), x + 1, z),
        ((x == wide_x - 1) & (z < deep_z - 1), x, z + 1),
        ((z > 0) & (x > 0), x - 1, z),
    ]
    second = [
        ((x == 0) & (z < deep_z - 1), x, z + 1),
        ((z > 0) & (x < wide_x - 1), x + 1, z),
        ((z == 1) & (x > 0), x, z - 1),
    ]
    return first, second


def spread_kernel(n_row, n_col, count, a_ref, pr, pn, zo, z, ra, rb, abuf,
                  in_sem, a_sem, p_send, p_recv, n_send, n_recv, s_send, s_recv):
    r, c = lax.axis_index("row"), lax.axis_index("col")
    wide_x, deep_z = n_col // n_row, n_row
    x, zz = lax.rem(c, wide_x), c // wide_x
    m, n = a_ref.shape
    rows = m // (2 * count)
    half = m // 2
    deep_y = n_row // 2
    y, core = r // 2, lax.rem(r, 2)
    greet(cross(r, c, n_row, n_col))

    kids = trees(x, zz, wide_x, deep_z)

    def piece(tree, i):
        return pr.at[pl.ds(pl.multiple_of(tree * half + i * rows, rows), rows), :]

    def p_copy(tree, kid, i, there):
        return pltpu.make_async_remote_copy(
            src_ref=piece(tree, i), dst_ref=piece(tree, i),
            send_sem=p_send.at[tree, kid, i], recv_sem=p_recv.at[tree, i],
            device_id=(r, there), device_id_type=MESH)

    def forward(tree, i):
        for k, (some, kx, kz) in enumerate(kids[tree]):
            @pl.when(some)
            def _():
                p_copy(tree, k, i, kz * wide_x + kx).start()

    def a_copies(i, slot):
        return [pltpu.make_async_copy(
            a_ref.at[pl.ds(pl.multiple_of(tree * half + i * rows, rows), rows), :],
            abuf.at[slot, pl.ds(tree * rows, rows), :], a_sem.at[slot, tree]) for tree in range(2)]

    for copy in a_copies(0, 0):
        copy.start()

    @pl.when(c == 0)
    def _():
        own = pltpu.make_async_copy(a_ref.at[:, pl.ds(0, NB)], pr, in_sem.at[0])
        own.start()
        own.wait()

        @pl.when(r == 0)
        def _():
            pr[pl.ds(0, NB), :] = jnp.zeros((NB, NB), F32)

        @pl.loop(0, count)
        def _(i):
            forward(0, i)
            forward(1, i)

    def n_copy(kid, there):
        return pltpu.make_async_remote_copy(
            src_ref=pn, dst_ref=pn, send_sem=n_send.at[kid], recv_sem=n_recv.at[0],
            device_id=(there, c), device_id_type=MESH)

    def n_forward():
        @pl.when(y < deep_y - 1)
        def _():
            n_copy(0, r + 2).start()
        n_copy(1, r + 1).start()

    @pl.when(r == 0)
    def _():
        own = pltpu.make_async_copy(a_ref.at[pl.ds(0, 2 * NB), :], pn, in_sem.at[1])
        own.start()
        own.wait()

        @pl.when(c == 0)
        def _():
            pn[pl.ds(0, NB), pl.ds(0, NB)] = jnp.zeros((NB, NB), F32)
        n_forward()

    z[...] = jnp.zeros_like(z)
    tile = min(n, 512)

    @pl.loop(0, count)
    def _(i):
        slot = lax.rem(i, 2)

        @pl.when(i + 1 < count)
        def _():
            for copy in a_copies(i + 1, 1 - slot):
                copy.start()

        @pl.when(c != 0)
        def _():
            for tree in range(2):
                p_copy(tree, 0, i, c).wait_recv()
                forward(tree, i)
        for copy in a_copies(i, slot):
            copy.wait()
        part = jnp.concatenate([piece(0, i)[...], piece(1, i)[...]])
        turned = part.T
        high_low = halves(turned)
        for at in range(0, n, tile):
            cut = pl.ds(at, tile)
            z[:, cut] += dot3(high_low, halves(abuf[slot, :, cut]))
        z[:, pl.ds(n, NB)] += exact(turned, part)

    @pl.when(r == 0)
    def _():
        z[:, pl.ds(n + NB, NB)] = pr[pl.ds(NB, NB), :]

    width = n + 2 * NB
    side = width // 2
    cut = side // deep_y
    mine = pl.multiple_of(core * side, LANES)
    other = pl.multiple_of((1 - core) * side, LANES)
    mate = (y * 2 + 1 - core, c)
    to_mate = pltpu.make_async_remote_copy(
        src_ref=z.at[:, pl.ds(other, side)], dst_ref=ra, send_sem=s_send.at[0], recv_sem=s_recv.at[0],
        device_id=mate, device_id_type=MESH)
    to_mate.start()

    @pl.when((r != 0) & (core == 0))
    def _():
        n_copy(0, r).wait_recv()
        n_forward()

    to_mate.wait_recv()
    z[:, pl.ds(mine, side)] += ra[...]
    out = []
    for k in range(1, deep_y):
        there = lax.rem(y + k, deep_y)
        copy = pltpu.make_async_remote_copy(
            src_ref=z.at[:, pl.ds(pl.multiple_of(mine + there * cut, LANES), cut)], dst_ref=rb.at[k - 1],
            send_sem=s_send.at[1 + k], recv_sem=s_recv.at[1 + k],
            device_id=(there * 2 + core, c), device_id_type=MESH)
        copy.start()
        out.append(copy)
    place = pl.ds(pl.multiple_of(mine + y * cut, LANES), cut)
    total = z[:, place]
    for k in range(1, deep_y):
        out[k - 1].wait_recv()
        total = total + rb[k - 1]
    zo[:, place] = total
    back = []
    for k in range(1, deep_y):
        there = lax.rem(y + k, deep_y)
        came = lax.rem(y - k + deep_y, deep_y)
        sent = pltpu.make_async_remote_copy(
            src_ref=zo.at[:, place], dst_ref=zo.at[:, place],
            send_sem=s_send.at[1 + deep_y + k], recv_sem=s_recv.at[1 + deep_y + k],
            device_id=(there * 2 + core, c), device_id_type=MESH)
        spot = pl.ds(pl.multiple_of(mine + came * cut, LANES), cut)
        got = pltpu.make_async_remote_copy(
            src_ref=zo.at[:, spot], dst_ref=zo.at[:, spot],
            send_sem=s_send.at[1 + deep_y + k], recv_sem=s_recv.at[1 + deep_y + k],
            device_id=(there * 2 + core, c), device_id_type=MESH)
        sent.start()
        back.append((sent, got))
    for _, got in back:
        got.wait_recv()
    swap = pltpu.make_async_remote_copy(
        src_ref=zo.at[:, pl.ds(mine, side)], dst_ref=zo.at[:, pl.ds(mine, side)],
        send_sem=s_send.at[1], recv_sem=s_recv.at[1], device_id=mate, device_id_type=MESH)
    swap_in = pltpu.make_async_remote_copy(
        src_ref=zo.at[:, pl.ds(other, side)], dst_ref=zo.at[:, pl.ds(other, side)],
        send_sem=s_send.at[1], recv_sem=s_recv.at[1], device_id=mate, device_id_type=MESH)
    swap.start()
    swap_in.wait_recv()

    @pl.when(core == 1)
    def _():
        n_copy(1, r).wait_recv()

    to_mate.wait_send()
    swap.wait_send()
    for copy in out:
        copy.wait_send()
    for sent, _ in back:
        sent.wait_send()

    @pl.when((core == 0) & (y < deep_y - 1))
    def _():
        n_copy(0, r).wait_send()

    @pl.when(core == 0)
    def _():
        n_copy(1, r).wait_send()

    for tree in range(2):
        for k, (some, _, _) in enumerate(kids[tree]):
            @pl.when(some)
            def _():
                @pl.loop(0, count)
                def _(i):
                    p_copy(tree, k, i, c).wait_send()


def spread(matrix, n_row, n_col):
    m, n = matrix.shape
    count = 16
    width = n + 2 * NB
    side = width // 2
    deep_y = n_row // 2
    rows = m // (2 * count)
    dma = pltpu.SemaphoreType.DMA
    vmem = pl.BlockSpec(memory_space=pltpu.VMEM)
    return pl.pallas_call(
        functools.partial(spread_kernel, n_row, n_col, count),
        out_shape=[
            jax.ShapeDtypeStruct((m, NB), F32),
            jax.ShapeDtypeStruct((2 * NB, n), F32),
            jax.ShapeDtypeStruct((NB, width), F32),
        ],
        in_specs=[pl.BlockSpec(memory_space=pl.ANY)],
        out_specs=[vmem] * 3,
        scratch_shapes=[
            pltpu.VMEM((NB, width), F32),
            pltpu.VMEM((NB, side), F32),
            pltpu.VMEM((max(deep_y - 1, 1), NB, side // deep_y), F32),
            pltpu.VMEM((2, 2 * rows, n), F32),
            dma((2,)), dma((2, 2)),
            dma((2, 3, count)), dma((2, count)),
            dma((2,)), dma((1,)),
            dma((2 + 2 * deep_y,)), dma((2 + 2 * deep_y,)),
        ],
        compiler_params=pltpu.CompilerParams(
            collective_id=0, has_side_effects=True, vmem_limit_bytes=48 * 1024 * 1024),
        cost_estimate=pl.CostEstimate(flops=6 * m * n * NB, bytes_accessed=4 * m * n, transcendentals=0),
        name="spread",
    )(matrix)


def gather_kernel(n_row, n_col, count, xc, part_ref, xr, inner, acc,
                  in_sem, z_send, x_send, x_recv, i_send, i_recv, b_send, b_recv, slots):
    r, c = lax.axis_index("row"), lax.axis_index("col")
    wide_x = n_col // n_row
    x, zz = lax.rem(c, wide_x), c // wide_x
    n = xc.shape[0]
    rows = n // count
    greet(cross(r, c, n_row, n_col))
    strip = NB // n_row
    own_strip = pl.ds(pl.multiple_of(r * strip, 8), strip)
    small = []
    for k in range(1, n_col):
        copy = pltpu.make_async_remote_copy(
            src_ref=part_ref.at[own_strip, :], dst_ref=slots.at[k - 1],
            send_sem=i_send.at[k - 1], recv_sem=i_recv.at[k - 1],
            device_id=(r, lax.rem(c + k, n_col)), device_id_type=MESH)
        copy.start()
        small.append(copy)

    def piece(block, i):
        return xr.at[pl.ds(pl.multiple_of(block * n + i * rows, rows), rows), :]

    def copy_to(block, i, sems, there):
        return pltpu.make_async_remote_copy(
            src_ref=piece(block, i), dst_ref=piece(block, i), send_sem=sems, recv_sem=x_recv.at[block, i],
            device_id=(r, there), device_id_type=MESH)

    @pl.when(zz == r)
    def _():
        own = pltpu.make_async_copy(xc, xr.at[pl.ds(pl.multiple_of(x * n, n), n), :], in_sem.at[0])
        own.start()
        own.wait()

    up = (zz >= r) & (zz < n_row - 1)
    down = (zz <= r) & (zz > 0)

    @pl.loop(0, count)
    def _(i):
        @pl.when(zz != r)
        def _():
            copy_to(x, i, z_send.at[0, i], c).wait_recv()

        @pl.when(up)
        def _():
            copy_to(x, i, z_send.at[0, i], c + wide_x).start()

        @pl.when(down)
        def _():
            copy_to(x, i, z_send.at[1, i], c - wide_x).start()

        @pl.when(x < wide_x - 1)
        def _():
            copy_to(x, i, x_send.at[0, x, i], c + 1).start()

        @pl.when(x > 0)
        def _():
            copy_to(x, i, x_send.at[1, x, i], c - 1).start()

        for block in range(wide_x):
            @pl.when(block != x)
            def _():
                copy_to(block, i, x_send.at[0, block, i], c).wait_recv()

            @pl.when((block < x) & (x < wide_x - 1))
            def _():
                copy_to(block, i, x_send.at[0, block, i], c + 1).start()

            @pl.when((block > x) & (x > 0))
            def _():
                copy_to(block, i, x_send.at[1, block, i], c - 1).start()

    total = part_ref[own_strip, :]
    for k in range(1, n_col):
        small[k - 1].wait_recv()
        total = total + slots[k - 1]
    inner[own_strip, :] = total
    last = []
    for k in range(1, n_row):
        there = lax.rem(r + k, n_row)
        came = lax.rem(r - k + n_row, n_row)
        sent = pltpu.make_async_remote_copy(
            src_ref=inner.at[own_strip, :], dst_ref=inner.at[own_strip, :],
            send_sem=b_send.at[k - 1], recv_sem=b_recv.at[k - 1],
            device_id=(there, c), device_id_type=MESH)
        spot = pl.ds(pl.multiple_of(came * strip, 8), strip)
        got = pltpu.make_async_remote_copy(
            src_ref=inner.at[spot, :], dst_ref=inner.at[spot, :],
            send_sem=b_send.at[k - 1], recv_sem=b_recv.at[k - 1],
            device_id=(there, c), device_id_type=MESH)
        sent.start()
        last.append((sent, got))
    for _, got in last:
        got.wait_recv()
    for sent, _ in last:
        sent.wait_send()
    for copy in small:
        copy.wait_send()

    def drain(some, block, sems):
        @pl.when(some)
        def _():
            @pl.loop(0, count)
            def _(i):
                copy_to(block, i, sems(i), c).wait_send()

    drain(up, 0, lambda i: z_send.at[0, i])
    drain(down, 0, lambda i: z_send.at[1, i])
    for block in range(wide_x):
        drain((block <= x) & (x < wide_x - 1), block, lambda i: x_send.at[0, block, i])
        drain((block >= x) & (x > 0), block, lambda i: x_send.at[1, block, i])


def gather(xc, part, n_row, n_col):
    n = xc.shape[0]
    count = 16
    wide_x = n_col // n_row
    dma = pltpu.SemaphoreType.DMA
    vmem = pl.BlockSpec(memory_space=pltpu.VMEM)
    return pl.pallas_call(
        functools.partial(gather_kernel, n_row, n_col, count),
        out_shape=[
            jax.ShapeDtypeStruct((wide_x * n, NB), F32),
            jax.ShapeDtypeStruct((NB, NB), F32),
        ],
        in_specs=[vmem] * 2,
        out_specs=[vmem] * 2,
        scratch_shapes=[
            pltpu.VMEM((8, LANES), F32),
            dma((1,)), dma((2, count)), dma((2, wide_x, count)), dma((wide_x, count)),
            dma((n_col - 1,)), dma((n_col - 1,)), dma((n_row - 1,)), dma((n_row - 1,)),
            pltpu.VMEM((n_col - 1, NB // n_row, NB), F32),
        ],
        compiler_params=pltpu.CompilerParams(
            collective_id=1, has_side_effects=True, vmem_limit_bytes=32 * 1024 * 1024),
        name="gather",
    )(xc, part)


def body(matrix):
    row_count, col_count = matrix.shape
    n_row, n_col = lax.axis_size("row"), lax.axis_size("col")
    share = row_count // n_col
    r, c = lax.axis_index("row"), lax.axis_index("col")
    panel_rows, heads, sums = spread(matrix, n_row, n_col)
    panel_cols, next_cols = heads[:NB], heads[NB:]
    y_cols = sums[:, :col_count]
    gram, top = sums[:, col_count : col_count + NB], sums[:, col_count + NB :]
    rinvt, linv, shape, low, tft = factor(gram, top)

    x_cols = exact(linv, exact(rinvt, y_cols) + next_cols)
    refl_cols = split3(shape, panel_cols, ((0,), (0,)))
    col_ids = jnp.arange(col_count)[None, :]
    in_top = (c == 0) & (col_ids >= NB) & (col_ids < 2 * NB)
    padded = jnp.zeros_like(refl_cols).at[:, NB : 2 * NB].set(low.T)
    refl_cols = jnp.where(in_top, padded, refl_cols)
    part = exact(refl_cols, x_cols, ((1,), (1,)))
    x_rows, inner = gather(x_cols.T, part, n_row, n_col)
    half = 0.5 * exact(tft, inner)

    refl_rows = split3(panel_rows, shape)
    row_ids = jnp.arange(row_count)[:, None]
    in_top = (r == 0) & (row_ids >= NB) & (row_ids < 2 * NB)
    padded = jnp.zeros_like(refl_rows).at[NB : 2 * NB].set(low)
    refl_rows = jnp.where(in_top, padded, refl_rows)
    w_rows = x_rows - split3(refl_rows, half)
    w_cols = x_cols - split3(half, refl_cols, ((0,), (0,)))
    left = jnp.concatenate([refl_rows, w_rows], axis=1)
    right = jnp.concatenate([w_cols, refl_cols], axis=0)
    updated = matrix - split3(left, right)
    v_out = lax.dynamic_slice_in_dim(refl_rows, c * share, share, 0)
    w_out = lax.dynamic_slice_in_dim(w_rows, c * share, share, 0)
    return updated, v_out[None], w_out[None]


def solution(mesh):
    return jax.shard_map(
        body,
        mesh=mesh,
        in_specs=(P("row", "col"),),
        out_specs=(P("row", "col"), P(None, ("row", "col"), None), P(None, ("row", "col"), None)),
        check_vma=False,
    )
```

```python
import functools

import jax
import jax.numpy as jnp
from jax import lax
from jax.experimental import pallas as pl
from jax.experimental.pallas import tpu as pltpu
from jax.sharding import PartitionSpec as P

NB = 256
STRIP = 16
LANES = 128
MESH = pl.DeviceIdType.MESH
F32 = jnp.float32
BF16 = jnp.bfloat16


def exact(left, right, dims=((1,), (0,))):
    return lax.dot_general(
        left, right, (dims, ((), ())),
        precision=lax.Precision.HIGHEST, preferred_element_type=F32,
    )


def split3(left, right, dims=((1,), (0,))):
    return lax.dot_general(
        left, right, (dims, ((), ())),
        precision=lax.Precision.HIGH, preferred_element_type=F32,
    )


def halves(value):
    high = value.astype(BF16)
    return high, (value - high.astype(F32)).astype(BF16)


def dot(left, right, dims=((1,), (0,))):
    return lax.dot_general(left, right, (dims, ((), ())), preferred_element_type=F32)


def dot3(left, right, dims=((1,), (0,))):
    (lh, ll), (rh, rl) = left, right
    return dot(lh, rh, dims) + (dot(lh, rl, dims) + dot(ll, rh, dims))


def wide(part, n):
    return jnp.concatenate([part] * (n // part.shape[1]), axis=1)


FACTOR_SCRATCH = 7


def factor_scratch(n):
    return [pltpu.VMEM((n, n), F32)] * FACTOR_SCRATCH + [pltpu.VMEM((n, LANES), F32)]


def factor_body(gram, top, rinvt_out, linv_out, shape_out, low_out, tft_out,
                wg, wt, fg, ft, lead, bd, bl, sg):
    n = gram.shape[0]
    strip = STRIP
    lanes = lax.broadcasted_iota(jnp.int32, (strip, n), 1)
    subs = lax.broadcasted_iota(jnp.int32, (strip, n), 0)
    lane = lax.broadcasted_iota(jnp.int32, (1, n), 1)
    subs1 = lax.broadcasted_iota(jnp.int32, (strip, LANES), 0)
    full = lax.broadcasted_iota(jnp.int32, (n, n), 1)
    wg[...] = gram
    wt[...] = top
    lead[...] = jnp.zeros_like(lead)

    def one(s, carry):
        at = pl.ds(pl.multiple_of(s * strip, strip), strip)
        g, t = wg[at, :], wt[at, :]
        keep = n - s * strip
        gc = [jnp.broadcast_to(g[:, j : j + 1], (strip, LANES)) for j in range(strip)]
        tc = [jnp.broadcast_to(t[:, j : j + 1], (strip, LANES)) for j in range(strip)]
        gf, tf, ld = g, t, jnp.where(lanes == subs, 1.0, 0.0)
        signs = jnp.zeros((strip, LANES), F32)
        for k in range(strip):
            gcol, gp = gc[k], gc[k][k : k + 1]
            root = 1.0 / jnp.sqrt(gp)
            ginv = root * root
            tcol, tp = tc[k], tc[k][k : k + 1]
            sign = jnp.where(tp >= 0, 1.0, -1.0)
            add = sign * root
            tinv = 1.0 / (tp + add * gp)
            grow = g[k : k + 1]
            trow = t[k : k + 1] + jnp.where((lane >= k) & (lane < keep), grow, 0.0) * wide(add, n)
            gf = jnp.where(subs == k, grow, gf)
            tf = jnp.where(subs == k, trow, tf)
            signs = jnp.where(subs1 == k, sign, signs)
            gscaled = jnp.where(lane == k, wide(ginv, n), grow * wide(ginv, n))
            tscaled = jnp.where(lane == k, wide(tinv, n), trow * wide(tinv, n))
            ld = jnp.where((lanes == k) & (subs > k), wide(tcol * tinv, n), ld)
            for j in range(k + 1, strip):
                grj = gc[j][k : k + 1]
                trj = (tc[j][k : k + 1] + add * grj) * tinv
                grj = grj * ginv
                gc[j] = jnp.where(subs1 == k, grj, gc[j] - gcol * grj)
                tc[j] = jnp.where(subs1 == k, trj, tc[j] - tcol * trj)
            g = jnp.where(subs == k, gscaled, jnp.where(lanes == k, 0.0, g) - wide(gcol, n) * gscaled)
            t = jnp.where(subs == k, tscaled, jnp.where(lanes == k, 0.0, t) - wide(tcol, n) * tscaled)
        back = s * strip
        fg[at, :] = pltpu.roll(gf, back, 1)
        ft[at, :] = pltpu.roll(tf, back, 1)
        bl[at, :] = pltpu.roll(ld, back, 1)
        bd[at, :] = pltpu.roll(jnp.where(lanes < strip, t, 0.0), back, 1)
        sg[at, :] = signs
        gw, tw = wg[...], wt[...]
        step = n - strip
        lead[...] = pltpu.roll(jnp.where(full < strip, tw, lead[...]), step, 1)
        gn = jnp.where(full < strip, 0.0, gw) - exact(gw[:, :strip], g)
        tn = jnp.where(full < strip, 0.0, tw) - exact(tw[:, :strip], t)
        wg[...] = pltpu.roll(gn, step, 1)
        wt[...] = pltpu.roll(tn, step, 1)
        wg[at, :] = pltpu.roll(g, step, 1)
        wt[at, :] = pltpu.roll(t, step, 1)
        return carry

    lax.fori_loop(0, n // strip, one, 0)
    rows = lax.broadcasted_iota(jnp.int32, (n, n), 0)
    cols = lax.broadcasted_iota(jnp.int32, (n, n), 1)
    eye = jnp.where(rows == cols, 1.0, 0.0)
    diag = jnp.sum(fg[...] * eye, axis=1, keepdims=True)
    rinvt = jnp.where(rows > cols, fg[...], eye) * (1.0 / jnp.sqrt(diag)) * wide(sg[...], n)
    linv = jnp.where(rows > cols, ft[...], eye)
    upper = jnp.where(rows <= cols, ft[...], 0.0)
    rinvt_out[...] = rinvt
    linv_out[...] = linv
    tft_out[...] = exact(linv, exact(rinvt, upper, ((1,), (1,))))
    low = exact(exact(jnp.where(rows >= cols - cols % strip, lead[...], 0.0), bd[...]), bl[...])
    low = jnp.where(rows > cols, low, eye)
    low_out[...] = low
    shape_out[...] = jnp.where(rows <= cols, exact(wt[...], low), 0.0)


def greet(partners):
    barrier = pltpu.get_barrier_semaphore()
    for device in partners:
        pl.semaphore_signal(barrier, inc=1, device_id=device, device_id_type=MESH)
    pl.semaphore_wait(barrier, len(partners))


def cross(r, c, n_row, n_col):
    return ([(lax.rem(r + k, n_row), c) for k in range(1, n_row)]
            + [(r, lax.rem(c + k, n_col)) for k in range(1, n_col)])


def trees(x, z, wide_x, deep_z):
    first = [
        ((z == 0) & (x < wide_x - 1), x + 1, z),
        ((x == wide_x - 1) & (z < deep_z - 1), x, z + 1),
        ((z > 0) & (x > 0), x - 1, z),
    ]
    second = [
        ((x == 0) & (z < deep_z - 1), x, z + 1),
        ((z > 0) & (x < wide_x - 1), x + 1, z),
        ((z == 1) & (x > 0), x, z - 1),
    ]
    return first, second


FACTORS = 6
ROWS = 128


def depths(x, z, wide_x):
    first = jnp.where(z == 0, x, 2 * (wide_x - 1) + z - x)
    second = jnp.where((z == 0) & (x > 0), x + 2, z + x)
    return first, second


def spread_kernel(n_row, n_col, count, extra, a_ref, pr, pn, zo, fac, z, ra, rb, abuf, gbuf, *rest):
    scratch, sems = rest[: FACTOR_SCRATCH + 1], rest[FACTOR_SCRATCH + 1 :]
    in_sem, a_sem, p_send, p_recv, n_send, n_recv, s_send, s_recv, g_send, g_recv, f_send, f_recv = sems
    r, c = lax.axis_index("row"), lax.axis_index("col")
    wide_x, deep_z = n_col // n_row, n_row
    x, zz = lax.rem(c, wide_x), c // wide_x
    m, n = a_ref.shape
    rows = ROWS
    half = m // 2
    deep_y = n_row // 2
    y, core = r // 2, lax.rem(r, 2)
    mate = (y * 2 + 1 - core, c)
    greet(cross(r, c, n_row, n_col))

    kids = trees(x, zz, wide_x, deep_z)
    depth = depths(x, zz, wide_x)
    total = count + extra

    def piece(tree, i):
        return pr.at[pl.ds(pl.multiple_of(tree * half + i * rows, rows), rows), :]

    def fact(side, tree, i):
        return fac.at[pl.ds(pl.multiple_of(((side * 2 + tree) * extra + i - count) * rows, rows), rows), :]

    def p_copy(tree, kid, i, there, ref):
        return pltpu.make_async_remote_copy(
            src_ref=ref, dst_ref=ref,
            send_sem=p_send.at[tree, kid, i], recv_sem=p_recv.at[tree, i],
            device_id=(r, there), device_id_type=MESH)

    def forward(tree, i, ref):
        for k, (some, kx, kz) in enumerate(kids[tree]):
            @pl.when(some)
            def _():
                p_copy(tree, k, i, kz * wide_x + kx, ref).start()

    def f_copy(side, tree, i):
        ref = fact(side, tree, i)
        return pltpu.make_async_remote_copy(
            src_ref=ref, dst_ref=ref, send_sem=f_send.at[tree, i - count], recv_sem=f_recv.at[tree, i - count],
            device_id=mate, device_id_type=MESH)

    def a_copies(i, slot):
        return [pltpu.make_async_copy(
            a_ref.at[pl.ds(pl.multiple_of(tree * half + i * rows, rows), rows), :],
            abuf.at[slot, pl.ds(tree * rows, rows), :], a_sem.at[slot, tree]) for tree in range(2)]

    for copy in a_copies(0, 0):
        copy.start()
    z[...] = jnp.zeros_like(z)
    tile = min(n, 512)

    def multiply(i):
        slot = lax.rem(i, 2)

        @pl.when(i + 1 < count)
        def _():
            for copy in a_copies(i + 1, 1 - slot):
                copy.start()
        for copy in a_copies(i, slot):
            copy.wait()
        part = jnp.concatenate([piece(0, i)[...], piece(1, i)[...]])
        high_low = halves(part.T)
        for at in range(0, n, tile):
            cut = pl.ds(at, tile)
            z[:, cut] += dot3(high_low, halves(abuf[slot, :, cut]))

    def n_copy(kid, there):
        return pltpu.make_async_remote_copy(
            src_ref=pn, dst_ref=pn, send_sem=n_send.at[kid], recv_sem=n_recv.at[0],
            device_id=(there, c), device_id_type=MESH)

    def n_forward():
        @pl.when(y < deep_y - 1)
        def _():
            n_copy(0, r + 2).start()
        n_copy(1, r + 1).start()

    def g_copy(kind, slot, there, sem):
        return pltpu.make_async_remote_copy(
            src_ref=gbuf.at[kind], dst_ref=gbuf.at[slot], send_sem=g_send.at[sem], recv_sem=g_recv.at[sem],
            device_id=(there, c), device_id_type=MESH)

    @pl.when(r == 0)
    def _():
        own = pltpu.make_async_copy(a_ref.at[pl.ds(0, 2 * NB), :], pn, in_sem.at[1])
        own.start()
        own.wait()

        @pl.when(c == 0)
        def _():
            pn[pl.ds(0, NB), pl.ds(0, NB)] = jnp.zeros((NB, NB), F32)

        @pl.when(c != 0)
        def _():
            n_forward()

    @pl.when(c == 0)
    def _():
        own = pltpu.make_async_copy(a_ref.at[:, pl.ds(0, NB)], pr, in_sem.at[0])
        own.start()
        own.wait()

        @pl.when(r == 0)
        def _():
            pr[pl.ds(0, NB), :] = jnp.zeros((NB, NB), F32)
            gbuf[1] = pr[pl.ds(NB, NB), :]
            g_copy(1, 1, r + 1, 1).start()

        @pl.loop(0, count)
        def _(i):
            for tree in range(2):
                forward(tree, i, piece(tree, i))

        gbuf[0] = jnp.zeros((NB, NB), F32)

        @pl.loop(0, m // NB)
        def _(i):
            part = pr[pl.ds(pl.multiple_of(i * NB, NB), NB), :]
            gbuf[0] += exact(part.T, part)

        @pl.when(core == 0)
        def _():
            g_copy(0, 2, r + 1, 0).wait_recv()
            gbuf[0] += gbuf[2]
            for k in range(1, deep_y):
                g_copy(0, 2 + k, lax.rem(y + k, deep_y) * 2, 1 + k).start()
            add = gbuf[0]
            for k in range(1, deep_y):
                g_copy(0, 2 + k, r, 1 + k).wait_recv()
                add = add + gbuf[2 + k]
            gbuf[2 + deep_y] = add
            g_copy(2 + deep_y, 2 + deep_y, r + 1, 0).start()

            @pl.when(y > 0)
            def _():
                g_copy(1, 1, r + 1, 1).wait_recv()

        @pl.when(core == 1)
        def _():
            g_copy(0, 2, r - 1, 0).start()

            @pl.when(y == 0)
            def _():
                g_copy(1, 1, r, 1).wait_recv()
                for k in range(1, deep_y):
                    g_copy(1, 1, k * 2 + 1, 1 + k).start()

            @pl.when(y > 0)
            def _():
                g_copy(1, 1, r, 1 + y).wait_recv()
                g_copy(1, 1, r - 1, 1).start()
            g_copy(2 + deep_y, 2 + deep_y, r, 0).wait_recv()

        @pl.when(r == 0)
        def _():
            n_forward()

        outs = [fac.at[pl.ds(k * NB, NB), :] for k in range(5)]
        fac[pl.ds(5 * NB, NB), :] = jnp.zeros((NB, NB), F32)
        factor_body(gbuf[2 + deep_y], gbuf[1], *outs, *scratch)
        for e in range(extra):
            for tree in range(2):
                forward(tree, count + e, fact(core, tree, count + e))

        @pl.loop(0, count)
        def _(i):
            multiply(i)

        @pl.when(core == 0)
        def _():
            for k in range(1, deep_y):
                g_copy(0, 2 + k, r, 1 + k).wait_send()
            g_copy(2 + deep_y, 2 + deep_y, r + 1, 0).wait_send()

        @pl.when(core == 1)
        def _():
            g_copy(0, 2, r - 1, 0).wait_send()

            @pl.when(y == 0)
            def _():
                for k in range(1, deep_y):
                    g_copy(1, 1, k * 2 + 1, 1 + k).wait_send()

        @pl.when((r == 0) | ((y > 0) & (core == 1)))
        def _():
            g_copy(1, 1, r, 1).wait_send()

    @pl.when(c != 0)
    def _():
        late = jnp.maximum(depth[0], depth[1])

        @pl.loop(0, total + 2 * wide_x + deep_z - 3)
        def _(t):
            for tree in range(2):
                i = t - depth[tree]

                @pl.when((i >= 0) & (i < count))
                def _():
                    p_copy(tree, 0, i, c, piece(tree, i)).wait_recv()
                    forward(tree, i, piece(tree, i))

                @pl.when((i >= count) & (i < total))
                def _():
                    ref = fact(core, tree, i)
                    p_copy(tree, 0, i, c, ref).wait_recv()
                    forward(tree, i, ref)
                    f_copy(core, tree, i).start()

            p = t - late

            @pl.when((p >= 0) & (p < count))
            def _():
                multiply(p)

    side = n // 2
    cut = NB // deep_y
    mine = pl.multiple_of(core * side, LANES)
    other = pl.multiple_of((1 - core) * side, LANES)
    to_mate = pltpu.make_async_remote_copy(
        src_ref=z.at[:, pl.ds(other, side)], dst_ref=ra, send_sem=s_send.at[0], recv_sem=s_recv.at[0],
        device_id=mate, device_id_type=MESH)
    to_mate.start()

    @pl.when((r != 0) & (core == 0))
    def _():
        n_copy(0, r).wait_recv()
        n_forward()

    to_mate.wait_recv()
    z[:, pl.ds(mine, side)] += ra[...]
    def band(at):
        return pl.ds(pl.multiple_of(at * cut, cut), cut)

    out = []
    for k in range(1, deep_y):
        there = lax.rem(y + k, deep_y)
        copy = pltpu.make_async_remote_copy(
            src_ref=z.at[band(there), pl.ds(mine, side)], dst_ref=rb.at[k - 1],
            send_sem=s_send.at[1 + k], recv_sem=s_recv.at[1 + k],
            device_id=(there * 2 + core, c), device_id_type=MESH)
        copy.start()
        out.append(copy)
    added = z[band(y), pl.ds(mine, side)]
    for k in range(1, deep_y):
        out[k - 1].wait_recv()
        added = added + rb[k - 1]
    zo[band(y), pl.ds(mine, side)] = added
    back = []
    for k in range(1, deep_y):
        there = lax.rem(y + k, deep_y)
        came = lax.rem(y - k + deep_y, deep_y)
        pair = [pltpu.make_async_remote_copy(
            src_ref=zo.at[band(where), pl.ds(mine, side)], dst_ref=zo.at[band(where), pl.ds(mine, side)],
            send_sem=s_send.at[1 + deep_y + k], recv_sem=s_recv.at[1 + deep_y + k],
            device_id=(there * 2 + core, c), device_id_type=MESH) for where in (y, came)]
        pair[0].start()
        back.append(pair)
    for _, got in back:
        got.wait_recv()
    swap, swap_in = [pltpu.make_async_remote_copy(
        src_ref=zo.at[:, pl.ds(at, side)], dst_ref=zo.at[:, pl.ds(at, side)],
        send_sem=s_send.at[1], recv_sem=s_recv.at[1], device_id=mate, device_id_type=MESH) for at in (mine, other)]
    swap.start()
    swap_in.wait_recv()

    @pl.when(core == 1)
    def _():
        n_copy(1, r).wait_recv()

    to_mate.wait_send()
    swap.wait_send()
    for copy in out:
        copy.wait_send()
    for sent, _ in back:
        sent.wait_send()

    @pl.when((core == 0) & (y < deep_y - 1))
    def _():
        n_copy(0, r).wait_send()

    @pl.when(core == 0)
    def _():
        n_copy(1, r).wait_send()

    @pl.when(c != 0)
    def _():
        for tree in range(2):
            for e in range(extra):
                f_copy(1 - core, tree, count + e).wait_recv()
                f_copy(core, tree, count + e).wait_send()

    for tree in range(2):
        for k, (some, _, _) in enumerate(kids[tree]):
            @pl.when(some)
            def _():
                @pl.loop(0, count)
                def _(i):
                    p_copy(tree, k, i, c, piece(tree, i)).wait_send()
                for e in range(extra):
                    p_copy(tree, k, count + e, c, fact(core, tree, count + e)).wait_send()


def spread(matrix, n_row, n_col):
    m, n = matrix.shape
    count = m // (2 * ROWS)
    extra = FACTORS * NB // (4 * ROWS)
    side = n // 2
    deep_y = n_row // 2
    dma = pltpu.SemaphoreType.DMA
    vmem = pl.BlockSpec(memory_space=pltpu.VMEM)
    return pl.pallas_call(
        functools.partial(spread_kernel, n_row, n_col, count, extra),
        out_shape=[
            jax.ShapeDtypeStruct((m, NB), F32),
            jax.ShapeDtypeStruct((2 * NB, n), F32),
            jax.ShapeDtypeStruct((NB, n), F32),
            jax.ShapeDtypeStruct((FACTORS * NB, NB), F32),
        ],
        in_specs=[pl.BlockSpec(memory_space=pl.ANY)],
        out_specs=[vmem] * 4,
        scratch_shapes=[
            pltpu.VMEM((NB, n), F32),
            pltpu.VMEM((NB, side), F32),
            pltpu.VMEM((max(deep_y - 1, 1), NB // deep_y, side), F32),
            pltpu.VMEM((2, 2 * ROWS, n), F32),
            pltpu.VMEM((3 + deep_y, NB, NB), F32),
            *factor_scratch(NB),
            dma((2,)), dma((2, 2)),
            dma((2, 3, count + extra)), dma((2, count + extra)),
            dma((2,)), dma((1,)),
            dma((2 + 2 * deep_y,)), dma((2 + 2 * deep_y,)),
            dma((1 + deep_y,)), dma((1 + deep_y,)),
            dma((2, extra)), dma((2, extra)),
        ],
        compiler_params=pltpu.CompilerParams(
            collective_id=0, has_side_effects=True, vmem_limit_bytes=48 * 1024 * 1024),
        cost_estimate=pl.CostEstimate(flops=6 * m * n * NB, bytes_accessed=4 * m * n, transcendentals=0),
        name="spread",
    )(matrix)


def gather_kernel(n_row, n_col, count, xc, part_ref, xr, inner, acc,
                  in_sem, z_send, x_send, x_recv, i_send, i_recv, b_send, b_recv, slots):
    r, c = lax.axis_index("row"), lax.axis_index("col")
    wide_x = n_col // n_row
    x, zz = lax.rem(c, wide_x), c // wide_x
    n = xc.shape[0]
    rows = n // count
    greet(cross(r, c, n_row, n_col))
    strip = NB // n_row
    own_strip = pl.ds(pl.multiple_of(r * strip, 8), strip)
    small = []
    for k in range(1, n_col):
        copy = pltpu.make_async_remote_copy(
            src_ref=part_ref.at[own_strip, :], dst_ref=slots.at[k - 1],
            send_sem=i_send.at[k - 1], recv_sem=i_recv.at[k - 1],
            device_id=(r, lax.rem(c + k, n_col)), device_id_type=MESH)
        copy.start()
        small.append(copy)

    def piece(block, i):
        return xr.at[pl.ds(pl.multiple_of(block * n + i * rows, rows), rows), :]

    def copy_to(block, i, sems, there):
        return pltpu.make_async_remote_copy(
            src_ref=piece(block, i), dst_ref=piece(block, i), send_sem=sems, recv_sem=x_recv.at[block, i],
            device_id=(r, there), device_id_type=MESH)

    @pl.when(zz == r)
    def _():
        own = pltpu.make_async_copy(xc, xr.at[pl.ds(pl.multiple_of(x * n, n), n), :], in_sem.at[0])
        own.start()
        own.wait()

    up = (zz >= r) & (zz < n_row - 1)
    down = (zz <= r) & (zz > 0)

    def take_own(i):
        @pl.when(zz != r)
        def _():
            copy_to(x, i, z_send.at[0, i], c).wait_recv()

        @pl.when(up)
        def _():
            copy_to(x, i, z_send.at[0, i], c + wide_x).start()

        @pl.when(down)
        def _():
            copy_to(x, i, z_send.at[1, i], c - wide_x).start()

        @pl.when(x < wide_x - 1)
        def _():
            copy_to(x, i, x_send.at[0, x, i], c + 1).start()

        @pl.when(x > 0)
        def _():
            copy_to(x, i, x_send.at[1, x, i], c - 1).start()

    @pl.loop(0, count + 2 * (wide_x - 1))
    def _(t):
        @pl.when(t < count)
        def _():
            take_own(t)

        for block in range(wide_x):
            i = t - 2 * jnp.abs(block - x)

            @pl.when((block != x) & (i >= 0) & (i < count))
            def _():
                copy_to(block, i, x_send.at[0, block, i], c).wait_recv()

                @pl.when((block < x) & (x < wide_x - 1))
                def _():
                    copy_to(block, i, x_send.at[0, block, i], c + 1).start()

                @pl.when((block > x) & (x > 0))
                def _():
                    copy_to(block, i, x_send.at[1, block, i], c - 1).start()

    total = part_ref[own_strip, :]
    for k in range(1, n_col):
        small[k - 1].wait_recv()
        total = total + slots[k - 1]
    inner[own_strip, :] = total
    last = []
    for k in range(1, n_row):
        there = lax.rem(r + k, n_row)
        came = lax.rem(r - k + n_row, n_row)
        sent = pltpu.make_async_remote_copy(
            src_ref=inner.at[own_strip, :], dst_ref=inner.at[own_strip, :],
            send_sem=b_send.at[k - 1], recv_sem=b_recv.at[k - 1],
            device_id=(there, c), device_id_type=MESH)
        spot = pl.ds(pl.multiple_of(came * strip, 8), strip)
        got = pltpu.make_async_remote_copy(
            src_ref=inner.at[spot, :], dst_ref=inner.at[spot, :],
            send_sem=b_send.at[k - 1], recv_sem=b_recv.at[k - 1],
            device_id=(there, c), device_id_type=MESH)
        sent.start()
        last.append((sent, got))
    for _, got in last:
        got.wait_recv()
    for sent, _ in last:
        sent.wait_send()
    for copy in small:
        copy.wait_send()

    def drain(some, block, sems):
        @pl.when(some)
        def _():
            @pl.loop(0, count)
            def _(i):
                copy_to(block, i, sems(i), c).wait_send()

    drain(up, 0, lambda i: z_send.at[0, i])
    drain(down, 0, lambda i: z_send.at[1, i])
    for block in range(wide_x):
        drain((block <= x) & (x < wide_x - 1), block, lambda i: x_send.at[0, block, i])
        drain((block >= x) & (x > 0), block, lambda i: x_send.at[1, block, i])


def gather(xc, part, n_row, n_col):
    n = xc.shape[0]
    count = 16
    wide_x = n_col // n_row
    dma = pltpu.SemaphoreType.DMA
    vmem = pl.BlockSpec(memory_space=pltpu.VMEM)
    return pl.pallas_call(
        functools.partial(gather_kernel, n_row, n_col, count),
        out_shape=[
            jax.ShapeDtypeStruct((wide_x * n, NB), F32),
            jax.ShapeDtypeStruct((NB, NB), F32),
        ],
        in_specs=[vmem] * 2,
        out_specs=[vmem] * 2,
        scratch_shapes=[
            pltpu.VMEM((8, LANES), F32),
            dma((1,)), dma((2, count)), dma((2, wide_x, count)), dma((wide_x, count)),
            dma((n_col - 1,)), dma((n_col - 1,)), dma((n_row - 1,)), dma((n_row - 1,)),
            pltpu.VMEM((n_col - 1, NB // n_row, NB), F32),
        ],
        compiler_params=pltpu.CompilerParams(
            collective_id=1, has_side_effects=True, vmem_limit_bytes=32 * 1024 * 1024),
        name="gather",
    )(xc, part)


def body(matrix):
    row_count, col_count = matrix.shape
    n_row, n_col = lax.axis_size("row"), lax.axis_size("col")
    share = row_count // n_col
    r, c = lax.axis_index("row"), lax.axis_index("col")
    panel_rows, heads, y_cols, fac = spread(matrix, n_row, n_col)
    panel_cols, next_cols = heads[:NB], heads[NB:]
    rinvt, linv, shape, low, tft = [fac[k * NB : (k + 1) * NB] for k in range(5)]

    x_cols = exact(linv, exact(rinvt, y_cols) + next_cols)
    refl_cols = split3(shape, panel_cols, ((0,), (0,)))
    col_ids = jnp.arange(col_count)[None, :]
    in_top = (c == 0) & (col_ids >= NB) & (col_ids < 2 * NB)
    padded = jnp.zeros_like(refl_cols).at[:, NB : 2 * NB].set(low.T)
    refl_cols = jnp.where(in_top, padded, refl_cols)
    part = exact(refl_cols, x_cols, ((1,), (1,)))
    x_rows, inner = gather(x_cols.T, part, n_row, n_col)
    half = 0.5 * exact(tft, inner)

    refl_rows = split3(panel_rows, shape)
    row_ids = jnp.arange(row_count)[:, None]
    in_top = (r == 0) & (row_ids >= NB) & (row_ids < 2 * NB)
    padded = jnp.zeros_like(refl_rows).at[NB : 2 * NB].set(low)
    refl_rows = jnp.where(in_top, padded, refl_rows)
    w_rows = x_rows - split3(refl_rows, half)
    w_cols = x_cols - split3(half, refl_cols, ((0,), (0,)))
    left = jnp.concatenate([refl_rows, w_rows], axis=1)
    right = jnp.concatenate([w_cols, refl_cols], axis=0)
    updated = matrix - split3(left, right)
    v_out = lax.dynamic_slice_in_dim(refl_rows, c * share, share, 0)
    w_out = lax.dynamic_slice_in_dim(w_rows, c * share, share, 0)
    return updated, v_out[None], w_out[None]


def solution(mesh):
    return jax.shard_map(
        body,
        mesh=mesh,
        in_specs=(P("row", "col"),),
        out_specs=(P("row", "col"), P(None, ("row", "col"), None), P(None, ("row", "col"), None)),
        check_vma=False,
    )
```

```python
import functools

import jax
import jax.numpy as jnp
from jax import lax
from jax.experimental import pallas as pl
from jax.experimental.pallas import tpu as pltpu
from jax.sharding import PartitionSpec as P

NB = 256
STRIP = 16
LANES = 128
MESH = pl.DeviceIdType.MESH
F32 = jnp.float32
BF16 = jnp.bfloat16


def exact(left, right, dims=((1,), (0,))):
    return lax.dot_general(
        left, right, (dims, ((), ())),
        precision=lax.Precision.HIGHEST, preferred_element_type=F32,
    )


def halves(value):
    high = value.astype(BF16)
    return high, (value - high.astype(F32)).astype(BF16)


def dot(left, right, dims=((1,), (0,))):
    return lax.dot_general(left, right, (dims, ((), ())), preferred_element_type=F32)


def dot3(left, right, dims=((1,), (0,))):
    (lh, ll), (rh, rl) = left, right
    return dot(lh, rh, dims) + (dot(lh, rl, dims) + dot(ll, rh, dims))


def wide(part, n):
    return jnp.concatenate([part] * (n // part.shape[1]), axis=1)


FACTOR_SCRATCH = 7


def factor_scratch(n):
    return [pltpu.VMEM((n, n), F32)] * FACTOR_SCRATCH + [pltpu.VMEM((n, LANES), F32)]


def factor_body(gram, top, rinvt_out, linv_out, shape_out, low_out, tft_out,
                wg, wt, fg, ft, lead, bd, bl, sg):
    n = gram.shape[0]
    strip = STRIP
    lanes = lax.broadcasted_iota(jnp.int32, (strip, n), 1)
    subs = lax.broadcasted_iota(jnp.int32, (strip, n), 0)
    lane = lax.broadcasted_iota(jnp.int32, (1, n), 1)
    subs1 = lax.broadcasted_iota(jnp.int32, (strip, LANES), 0)
    full = lax.broadcasted_iota(jnp.int32, (n, n), 1)
    wg[...] = gram
    wt[...] = top
    lead[...] = jnp.zeros_like(lead)

    def one(s, carry):
        at = pl.ds(pl.multiple_of(s * strip, strip), strip)
        g, t = wg[at, :], wt[at, :]
        keep = n - s * strip
        gc = [jnp.broadcast_to(g[:, j : j + 1], (strip, LANES)) for j in range(strip)]
        tc = [jnp.broadcast_to(t[:, j : j + 1], (strip, LANES)) for j in range(strip)]
        gf, tf, ld = g, t, jnp.where(lanes == subs, 1.0, 0.0)
        signs = jnp.zeros((strip, LANES), F32)
        for k in range(strip):
            gcol, gp = gc[k], gc[k][k : k + 1]
            root = 1.0 / jnp.sqrt(gp)
            ginv = root * root
            tcol, tp = tc[k], tc[k][k : k + 1]
            sign = jnp.where(tp >= 0, 1.0, -1.0)
            add = sign * root
            tinv = 1.0 / (tp + add * gp)
            grow = g[k : k + 1]
            trow = t[k : k + 1] + jnp.where((lane >= k) & (lane < keep), grow, 0.0) * wide(add, n)
            gf = jnp.where(subs == k, grow, gf)
            tf = jnp.where(subs == k, trow, tf)
            signs = jnp.where(subs1 == k, sign, signs)
            gscaled = jnp.where(lane == k, wide(ginv, n), grow * wide(ginv, n))
            tscaled = jnp.where(lane == k, wide(tinv, n), trow * wide(tinv, n))
            ld = jnp.where((lanes == k) & (subs > k), wide(tcol * tinv, n), ld)
            for j in range(k + 1, strip):
                grj = gc[j][k : k + 1]
                trj = (tc[j][k : k + 1] + add * grj) * tinv
                grj = grj * ginv
                gc[j] = jnp.where(subs1 == k, grj, gc[j] - gcol * grj)
                tc[j] = jnp.where(subs1 == k, trj, tc[j] - tcol * trj)
            g = jnp.where(subs == k, gscaled, jnp.where(lanes == k, 0.0, g) - wide(gcol, n) * gscaled)
            t = jnp.where(subs == k, tscaled, jnp.where(lanes == k, 0.0, t) - wide(tcol, n) * tscaled)
        back = s * strip
        fg[at, :] = pltpu.roll(gf, back, 1)
        ft[at, :] = pltpu.roll(tf, back, 1)
        bl[at, :] = pltpu.roll(ld, back, 1)
        bd[at, :] = pltpu.roll(jnp.where(lanes < strip, t, 0.0), back, 1)
        sg[at, :] = signs
        gw, tw = wg[...], wt[...]
        step = n - strip
        lead[...] = pltpu.roll(jnp.where(full < strip, tw, lead[...]), step, 1)
        gn = jnp.where(full < strip, 0.0, gw) - exact(gw[:, :strip], g)
        tn = jnp.where(full < strip, 0.0, tw) - exact(tw[:, :strip], t)
        wg[...] = pltpu.roll(gn, step, 1)
        wt[...] = pltpu.roll(tn, step, 1)
        wg[at, :] = pltpu.roll(g, step, 1)
        wt[at, :] = pltpu.roll(t, step, 1)
        return carry

    lax.fori_loop(0, n // strip, one, 0)
    rows = lax.broadcasted_iota(jnp.int32, (n, n), 0)
    cols = lax.broadcasted_iota(jnp.int32, (n, n), 1)
    eye = jnp.where(rows == cols, 1.0, 0.0)
    diag = jnp.sum(fg[...] * eye, axis=1, keepdims=True)
    rinvt = jnp.where(rows > cols, fg[...], eye) * (1.0 / jnp.sqrt(diag)) * wide(sg[...], n)
    linv = jnp.where(rows > cols, ft[...], eye)
    upper = jnp.where(rows <= cols, ft[...], 0.0)
    rinvt_out[...] = rinvt
    linv_out[...] = linv
    tft_out[...] = exact(linv, exact(rinvt, upper, ((1,), (1,))))
    low = exact(exact(jnp.where(rows >= cols - cols % strip, lead[...], 0.0), bd[...]), bl[...])
    low = jnp.where(rows > cols, low, eye)
    low_out[...] = low
    shape_out[...] = jnp.where(rows <= cols, exact(wt[...], low), 0.0)


def greet(partners):
    barrier = pltpu.get_barrier_semaphore()
    for device in partners:
        pl.semaphore_signal(barrier, inc=1, device_id=device, device_id_type=MESH)
    pl.semaphore_wait(barrier, len(partners))


def cross(r, c, n_row, n_col):
    return ([(lax.rem(r + k, n_row), c) for k in range(1, n_row)]
            + [(r, lax.rem(c + k, n_col)) for k in range(1, n_col)])


def trees(x, z, wide_x, deep_z):
    first = [
        ((z == 0) & (x < wide_x - 1), x + 1, z),
        ((x == wide_x - 1) & (z < deep_z - 1), x, z + 1),
        ((z > 0) & (x > 0), x - 1, z),
    ]
    second = [
        ((x == 0) & (z < deep_z - 1), x, z + 1),
        ((z > 0) & (x < wide_x - 1), x + 1, z),
        ((z == 1) & (x > 0), x, z - 1),
    ]
    return first, second


FACTORS = 6
ROWS = 64
DEEP = 128
SKEW = 2


def depths(x, z, wide_x):
    first = jnp.where(z == 0, x, 2 * (wide_x - 1) + z - x)
    second = jnp.where((z == 0) & (x > 0), x + 2, z + x)
    return first, second


def panel_kernel(n_row, n_col, count, extra, a_ref, vr, xr, rh, rl, v_out, w_out,
                 pr, pn, zo, fac, z, ra, rb, abuf, gbuf, xt, vt, inner, cross_sum, isrc, idst, *rest):
    scratch, sems = rest[: FACTOR_SCRATCH + 1], rest[FACTOR_SCRATCH + 1 :]
    (in_sem, a_sem, p_send, p_recv, n_send, n_recv, s_send, s_recv, g_send, g_recv, f_send, f_recv,
     z_send, x_send, x_recv, i_send, i_recv, b_send, b_recv) = sems
    r, c = lax.axis_index("row"), lax.axis_index("col")
    wide_x, deep_z = n_col // n_row, n_row
    x, zz = lax.rem(c, wide_x), c // wide_x
    m, n = a_ref.shape
    rows = ROWS
    half = m // 2
    deep_y = n_row // 2
    y, core = r // 2, lax.rem(r, 2)
    mate = (y * 2 + 1 - core, c)
    greet(cross(r, c, n_row, n_col))

    kids = trees(x, zz, wide_x, deep_z)
    depth = [SKEW * hops for hops in depths(x, zz, wide_x)]
    last_step = SKEW * (2 * wide_x + deep_z - 3)

    def piece(tree, i):
        return pr.at[pl.ds(pl.multiple_of(tree * half + i * rows, rows), rows), :]

    def fact(side, tree, i):
        return fac.at[pl.ds(pl.multiple_of(((side * 2 + tree) * extra + i - count) * rows, rows), rows), :]

    def p_copy(tree, kid, i, there, ref):
        return pltpu.make_async_remote_copy(
            src_ref=ref, dst_ref=ref,
            send_sem=p_send.at[tree, kid, i], recv_sem=p_recv.at[tree, i],
            device_id=(r, there), device_id_type=MESH)

    def forward(tree, i, ref):
        for k, (some, kx, kz) in enumerate(kids[tree]):
            @pl.when(some)
            def _():
                p_copy(tree, k, i, kz * wide_x + kx, ref).start()

    def f_copy(side, tree, i):
        ref = fact(side, tree, i)
        return pltpu.make_async_remote_copy(
            src_ref=ref, dst_ref=ref, send_sem=f_send.at[tree, i - count], recv_sem=f_recv.at[tree, i - count],
            device_id=mate, device_id_type=MESH)

    def deep(tree, i):
        return pl.ds(pl.multiple_of(tree * half + i * DEEP, DEEP), DEEP)

    def a_copies(i, slot):
        return [pltpu.make_async_copy(
            a_ref.at[deep(tree, i), :], abuf.at[slot, pl.ds(tree * DEEP, DEEP), :], a_sem.at[slot, tree])
            for tree in range(2)]

    for copy in a_copies(0, 0):
        copy.start()
    z[...] = jnp.zeros_like(z)
    tile = min(n, 512)

    def multiply(i):
        slot = lax.rem(i, 2)

        @pl.when(i + 1 < half // DEEP)
        def _():
            for copy in a_copies(i + 1, 1 - slot):
                copy.start()
        for copy in a_copies(i, slot):
            copy.wait()
        part = jnp.concatenate([pr[deep(0, i), :], pr[deep(1, i), :]])
        high_low = halves(part.T)
        for at in range(0, n, tile):
            cut = pl.ds(at, tile)
            z[:, cut] += dot3(high_low, halves(abuf[slot, :, cut]))

    def n_copy(kid, there):
        return pltpu.make_async_remote_copy(
            src_ref=pn, dst_ref=pn, send_sem=n_send.at[kid], recv_sem=n_recv.at[0],
            device_id=(there, c), device_id_type=MESH)

    def n_forward():
        @pl.when(y < deep_y - 1)
        def _():
            n_copy(0, r + 2).start()
        n_copy(1, r + 1).start()

    def g_copy(kind, slot, there, sem):
        return pltpu.make_async_remote_copy(
            src_ref=gbuf.at[kind], dst_ref=gbuf.at[slot], send_sem=g_send.at[sem], recv_sem=g_recv.at[sem],
            device_id=(there, c), device_id_type=MESH)

    @pl.when(c == 0)
    def _():
        own = pltpu.make_async_copy(a_ref.at[:, pl.ds(0, NB)], pr, in_sem.at[0])
        own.start()
        own.wait()

        @pl.when(r == 0)
        def _():
            pr[pl.ds(0, NB), :] = jnp.zeros((NB, NB), F32)
            gbuf[1] = pr[pl.ds(NB, NB), :]
            g_copy(1, 1, r + 1, 1).start()

        @pl.loop(0, count)
        def _(i):
            for tree in range(2):
                forward(tree, i, piece(tree, i))

    @pl.when(r == 0)
    def _():
        own = pltpu.make_async_copy(a_ref.at[pl.ds(0, 2 * NB), :], pn, in_sem.at[1])
        own.start()
        own.wait()

        @pl.when(c == 0)
        def _():
            pn[pl.ds(0, NB), pl.ds(0, NB)] = jnp.zeros((NB, NB), F32)

        @pl.when(c != 0)
        def _():
            n_forward()

    @pl.when(c == 0)
    def _():
        gbuf[0] = jnp.zeros((NB, NB), F32)

        @pl.loop(0, m // (4 * NB))
        def _(i):
            part = pr[pl.ds(pl.multiple_of(i * 4 * NB, NB), 4 * NB), :]
            gbuf[0] += exact(part.T, part)

        @pl.when(core == 0)
        def _():
            g_copy(0, 2, r + 1, 0).wait_recv()
            gbuf[0] += gbuf[2]
            for k in range(1, deep_y):
                g_copy(0, 2 + k, lax.rem(y + k, deep_y) * 2, 1 + k).start()
            add = gbuf[0]
            for k in range(1, deep_y):
                g_copy(0, 2 + k, r, 1 + k).wait_recv()
                add = add + gbuf[2 + k]
            gbuf[2 + deep_y] = add
            g_copy(2 + deep_y, 2 + deep_y, r + 1, 0).start()

            @pl.when(y > 0)
            def _():
                g_copy(1, 1, r + 1, 1).wait_recv()

        @pl.when(core == 1)
        def _():
            g_copy(0, 2, r - 1, 0).start()

            @pl.when(y == 0)
            def _():
                g_copy(1, 1, r, 1).wait_recv()
                for k in range(1, deep_y):
                    g_copy(1, 1, k * 2 + 1, 1 + k).start()

            @pl.when(y > 0)
            def _():
                g_copy(1, 1, r, 1 + y).wait_recv()
                g_copy(1, 1, r - 1, 1).start()
            g_copy(2 + deep_y, 2 + deep_y, r, 0).wait_recv()

        @pl.when(r == 0)
        def _():
            n_forward()

        outs = [fac.at[pl.ds(k * NB, NB), :] for k in range(5)]
        fac[pl.ds(5 * NB, NB), :] = jnp.zeros((NB, NB), F32)
        factor_body(gbuf[2 + deep_y], gbuf[1], *outs, *scratch)
        for e in range(extra):
            for tree in range(2):
                forward(tree, count + e, fact(core, tree, count + e))

        @pl.loop(0, half // DEEP)
        def _(i):
            multiply(i)

        @pl.when(core == 0)
        def _():
            for k in range(1, deep_y):
                g_copy(0, 2 + k, r, 1 + k).wait_send()
            g_copy(2 + deep_y, 2 + deep_y, r + 1, 0).wait_send()

        @pl.when(core == 1)
        def _():
            g_copy(0, 2, r - 1, 0).wait_send()

            @pl.when(y == 0)
            def _():
                for k in range(1, deep_y):
                    g_copy(1, 1, k * 2 + 1, 1 + k).wait_send()

        @pl.when((r == 0) | ((y > 0) & (core == 1)))
        def _():
            g_copy(1, 1, r, 1).wait_send()

    @pl.when(c != 0)
    def _():
        late = jnp.maximum(depth[0], depth[1])

        @pl.loop(0, count + last_step)
        def _(t):
            for tree in range(2):
                i = t - depth[tree]

                @pl.when((i >= 0) & (i < count))
                def _():
                    p_copy(tree, 0, i, c, piece(tree, i)).wait_recv()
                    forward(tree, i, piece(tree, i))

            p = t - late

            @pl.when((p >= 0) & (p < count) & (lax.rem(p, 2) == 1))
            def _():
                multiply(p // 2)

    def take_factors(first, last):
        @pl.when(c != 0)
        def _():
            @pl.loop(first, last)
            def _(t):
                for tree in range(2):
                    i = t - depth[tree]

                    @pl.when((i >= 0) & (i < extra))
                    def _():
                        ref = fact(core, tree, count + i)
                        p_copy(tree, 0, count + i, c, ref).wait_recv()
                        forward(tree, count + i, ref)
                        f_copy(core, tree, count + i).start()

    side = n // 2
    cut = NB // deep_y
    mine = pl.multiple_of(core * side, LANES)
    other = pl.multiple_of((1 - core) * side, LANES)
    to_mate = pltpu.make_async_remote_copy(
        src_ref=z.at[:, pl.ds(other, side)], dst_ref=ra, send_sem=s_send.at[0], recv_sem=s_recv.at[0],
        device_id=mate, device_id_type=MESH)
    to_mate.start()

    @pl.when((r != 0) & (core == 0))
    def _():
        n_copy(0, r).wait_recv()
        n_forward()

    to_mate.wait_recv()
    z[:, pl.ds(mine, side)] += ra[...]
    def band(at):
        return pl.ds(pl.multiple_of(at * cut, cut), cut)

    out = []
    for k in range(1, deep_y):
        there = lax.rem(y + k, deep_y)
        copy = pltpu.make_async_remote_copy(
            src_ref=z.at[band(there), pl.ds(mine, side)], dst_ref=rb.at[k - 1],
            send_sem=s_send.at[1 + k], recv_sem=s_recv.at[1 + k],
            device_id=(there * 2 + core, c), device_id_type=MESH)
        copy.start()
        out.append(copy)
    pause = extra + last_step // 2
    take_factors(0, pause)
    added = z[band(y), pl.ds(mine, side)]
    for k in range(1, deep_y):
        out[k - 1].wait_recv()
        added = added + rb[k - 1]
    zo[band(y), pl.ds(mine, side)] = added
    back = []
    for k in range(1, deep_y):
        there = lax.rem(y + k, deep_y)
        came = lax.rem(y - k + deep_y, deep_y)
        pair = [pltpu.make_async_remote_copy(
            src_ref=zo.at[band(where), pl.ds(mine, side)], dst_ref=zo.at[band(where), pl.ds(mine, side)],
            send_sem=s_send.at[1 + deep_y + k], recv_sem=s_recv.at[1 + deep_y + k],
            device_id=(there * 2 + core, c), device_id_type=MESH) for where in (y, came)]
        pair[0].start()
        back.append(pair)
    take_factors(pause, extra + last_step)
    for _, got in back:
        got.wait_recv()
    swap, swap_in = [pltpu.make_async_remote_copy(
        src_ref=zo.at[:, pl.ds(at, side)], dst_ref=zo.at[:, pl.ds(at, side)],
        send_sem=s_send.at[1], recv_sem=s_recv.at[1], device_id=mate, device_id_type=MESH) for at in (mine, other)]
    swap.start()
    swap_in.wait_recv()

    @pl.when(core == 1)
    def _():
        n_copy(1, r).wait_recv()

    @pl.when(c != 0)
    def _():
        for tree in range(2):
            for e in range(extra):
                f_copy(1 - core, tree, count + e).wait_recv()

    rinvt, linv, shape, tft, low = [fac.at[pl.ds(k * NB, NB), :] for k in (0, 1, 2, 4, 3)]

    x_count = n // ROWS
    own_block = pl.multiple_of(x * n, n)

    def x_piece(block, i):
        return xr.at[pl.ds(pl.multiple_of(block * n + i * ROWS, ROWS), ROWS), :]

    def x_copy(block, i, sem, there):
        return pltpu.make_async_remote_copy(
            src_ref=x_piece(block, i), dst_ref=x_piece(block, i), send_sem=sem, recv_sem=x_recv.at[block, i],
            device_id=(r, there), device_id_type=MESH)

    up = (zz >= r) & (zz < n_row - 1)
    down = (zz <= r) & (zz > 0)

    def take_own(i):
        @pl.when(zz != r)
        def _():
            x_copy(x, i, z_send.at[0, i], c).wait_recv()

        @pl.when(up)
        def _():
            x_copy(x, i, z_send.at[0, i], c + wide_x).start()

        @pl.when(down)
        def _():
            x_copy(x, i, z_send.at[1, i], c - wide_x).start()

        @pl.when(x < wide_x - 1)
        def _():
            x_copy(x, i, x_send.at[0, x, i], c + 1).start()

        @pl.when(x > 0)
        def _():
            x_copy(x, i, x_send.at[1, x, i], c - 1).start()

    for at in range(0, n, tile):
        cut_n = pl.ds(at, tile)
        value = exact(linv[...], exact(rinvt[...], zo[:, cut_n]) + pn[pl.ds(NB, NB), cut_n])
        xt[:, cut_n] = value

        @pl.when(zz == r)
        def _():
            xr[pl.ds(pl.multiple_of(own_block + at, tile), tile), :] = value.T
            for i in range(at // ROWS, (at + tile) // ROWS):
                take_own(i)

    shape_parts = halves(shape[...])
    shape_turned = halves(shape[...].T)
    ids = lax.broadcasted_iota(jnp.int32, (NB, NB), 0)
    for at in range(0, n, tile):
        cut_n = pl.ds(at, tile)
        vt[:, cut_n] = dot3(shape_turned, halves(pn[pl.ds(0, NB), cut_n]))

    @pl.when(c == 0)
    def _():
        vt[:, pl.ds(NB, NB)] = low[...].T
    inner[...] = jnp.zeros_like(inner)
    for at in range(0, n, tile):
        cut_n = pl.ds(at, tile)
        inner[...] += exact(vt[:, cut_n], xt[:, cut_n], ((1,), (1,)))

    strip = NB // n_row
    own_strip = pl.ds(pl.multiple_of(r * strip, 8), strip)
    mates = []
    step = 1
    while step < wide_x:
        mates.append(c + step * (1 - 2 * lax.rem(x // step, 2)))
        step *= 2
    step = 1
    while step < deep_z:
        mates.append(c + wide_x * step * (1 - 2 * lax.rem(zz // step, 2)))
        step *= 2
    stages = len(mates)

    def i_copy(k):
        return pltpu.make_async_remote_copy(
            src_ref=isrc.at[k], dst_ref=idst.at[k], send_sem=i_send.at[k], recv_sem=i_recv.at[k],
            device_id=(r, mates[k]), device_id_type=MESH)

    def b_copy(k, receive):
        at = lax.rem(r - k + n_row, n_row) if receive else r
        spot = cross_sum.at[pl.ds(pl.multiple_of(at * strip, 8), strip), :]
        return pltpu.make_async_remote_copy(
            src_ref=spot, dst_ref=spot, send_sem=b_send.at[k - 1], recv_sem=b_recv.at[k - 1],
            device_id=(lax.rem(r + k, n_row), c), device_id_type=MESH)

    isrc[0] = inner[own_strip, :]
    i_copy(0).start()

    @pl.loop(0, m // NB)
    def _(g):
        here = pl.ds(pl.multiple_of(g * NB, NB), NB)
        vr[here, :] = dot3(halves(pr[here, :]), shape_parts)

    @pl.when(r == 0)
    def _():
        vr[pl.ds(NB, NB), :] = low[...]

    depth_z = SKEW * jnp.abs(zz - r)

    @pl.loop(0, max(x_count + SKEW * (deep_z + wide_x - 2), 2 * stages + 4))
    def _(t):
        i_own = t - depth_z

        @pl.when((zz != r) & (i_own >= 0) & (i_own < x_count))
        def _():
            take_own(i_own)

        for block in range(wide_x):
            i = t - depth_z - SKEW * jnp.abs(block - x)

            @pl.when((block != x) & (i >= 0) & (i < x_count))
            def _():
                x_copy(block, i, x_send.at[0, block, i], c).wait_recv()

                @pl.when((block < x) & (x < wide_x - 1))
                def _():
                    x_copy(block, i, x_send.at[0, block, i], c + 1).start()

                @pl.when((block > x) & (x > 0))
                def _():
                    x_copy(block, i, x_send.at[1, block, i], c - 1).start()

        for k in range(stages):
            @pl.when(t == 2 * k + 1)
            def _():
                i_copy(k).wait_recv()
                if k + 1 < stages:
                    isrc[k + 1] = isrc[k] + idst[k]
                    i_copy(k + 1).start()
                else:
                    cross_sum[own_strip, :] = isrc[k] + idst[k]
                    for j in range(1, n_row):
                        b_copy(j, False).start()

        @pl.when(t == 2 * stages + 3)
        def _():
            for j in range(1, n_row):
                b_copy(j, True).wait_recv()
            half_h = 0.5 * exact(tft[...], cross_sum[...])
            gbuf[0] = half_h
            both = halves(half_h + half_h.T)
            for at in range(0, n, tile):
                cut_n = pl.ds(at, tile)
                v_parts = halves(vt[:, cut_n])
                g_parts = halves(xt[:, cut_n] - dot3(both, v_parts))
                rh[pl.ds(0, NB), cut_n], rl[pl.ds(0, NB), cut_n] = g_parts
                rh[pl.ds(NB, NB), cut_n], rl[pl.ds(NB, NB), cut_n] = v_parts

    share = m // n_col
    mine_rows = pl.ds(pl.multiple_of(c * share, 8), share)
    v_mine = vr[mine_rows, :]
    v_out[...] = v_mine
    w_out[...] = xr[mine_rows, :] - exact(v_mine, gbuf[0])

    for k in range(stages):
        i_copy(k).wait_send()
    for j in range(1, n_row):
        b_copy(j, False).wait_send()

    def drain(some, block, sems_of):
        @pl.when(some)
        def _():
            @pl.loop(0, x_count)
            def _(i):
                x_copy(block, i, sems_of(i), c).wait_send()

    drain(up, 0, lambda i: z_send.at[0, i])
    drain(down, 0, lambda i: z_send.at[1, i])
    for block in range(wide_x):
        drain((block <= x) & (x < wide_x - 1), block, lambda i: x_send.at[0, block, i])
        drain((block >= x) & (x > 0), block, lambda i: x_send.at[1, block, i])

    to_mate.wait_send()
    swap.wait_send()
    for copy in out:
        copy.wait_send()
    for sent, _ in back:
        sent.wait_send()

    @pl.when((core == 0) & (y < deep_y - 1))
    def _():
        n_copy(0, r).wait_send()

    @pl.when(core == 0)
    def _():
        n_copy(1, r).wait_send()

    @pl.when(c != 0)
    def _():
        for tree in range(2):
            for e in range(extra):
                f_copy(core, tree, count + e).wait_send()

    for tree in range(2):
        for k, (some, _, _) in enumerate(kids[tree]):
            @pl.when(some)
            def _():
                @pl.loop(0, count)
                def _(i):
                    p_copy(tree, k, i, c, piece(tree, i)).wait_send()
                for e in range(extra):
                    p_copy(tree, k, count + e, c, fact(core, tree, count + e)).wait_send()


def panel(matrix, n_row, n_col):
    m, n = matrix.shape
    count = m // (2 * ROWS)
    extra = FACTORS * NB // (4 * ROWS)
    side = n // 2
    deep_y = n_row // 2
    wide_x = n_col // n_row
    x_count = n // ROWS
    share = m // n_col
    stages = (wide_x.bit_length() - 1) + (n_row.bit_length() - 1)
    dma = pltpu.SemaphoreType.DMA
    vmem = pl.BlockSpec(memory_space=pltpu.VMEM)
    return pl.pallas_call(
        functools.partial(panel_kernel, n_row, n_col, count, extra),
        out_shape=[
            jax.ShapeDtypeStruct((m, NB), F32),
            jax.ShapeDtypeStruct((m, NB), F32),
            jax.ShapeDtypeStruct((2 * NB, n), BF16),
            jax.ShapeDtypeStruct((2 * NB, n), BF16),
            jax.ShapeDtypeStruct((share, NB), F32),
            jax.ShapeDtypeStruct((share, NB), F32),
        ],
        in_specs=[pl.BlockSpec(memory_space=pl.ANY)],
        out_specs=[vmem] * 6,
        scratch_shapes=[
            pltpu.VMEM((m, NB), F32),
            pltpu.VMEM((2 * NB, n), F32),
            pltpu.VMEM((NB, n), F32),
            pltpu.VMEM((FACTORS * NB, NB), F32),
            pltpu.VMEM((NB, n), F32),
            pltpu.VMEM((NB, side), F32),
            pltpu.VMEM((max(deep_y - 1, 1), NB // deep_y, side), F32),
            pltpu.VMEM((2, 2 * DEEP, n), F32),
            pltpu.VMEM((3 + deep_y, NB, NB), F32),
            pltpu.VMEM((NB, n), F32),
            pltpu.VMEM((NB, n), F32),
            pltpu.VMEM((NB, NB), F32),
            pltpu.VMEM((NB, NB), F32),
            pltpu.VMEM((stages, NB // n_row, NB), F32),
            pltpu.VMEM((stages, NB // n_row, NB), F32),
            *factor_scratch(NB),
            dma((2,)), dma((2, 2)),
            dma((2, 3, count + extra)), dma((2, count + extra)),
            dma((2,)), dma((1,)),
            dma((2 + 2 * deep_y,)), dma((2 + 2 * deep_y,)),
            dma((1 + deep_y,)), dma((1 + deep_y,)),
            dma((2, extra)), dma((2, extra)),
            dma((2, x_count)), dma((2, wide_x, x_count)), dma((wide_x, x_count)),
            dma((stages,)), dma((stages,)), dma((n_row - 1,)), dma((n_row - 1,)),
        ],
        compiler_params=pltpu.CompilerParams(
            collective_id=0, has_side_effects=True, vmem_limit_bytes=60 * 1024 * 1024),
        cost_estimate=pl.CostEstimate(flops=6 * m * n * NB, bytes_accessed=4 * m * n, transcendentals=0),
        name="panel",
    )(matrix)


def finish_kernel(a_ref, v_ref, x_ref, rh, rl, o_ref):
    n = a_ref.shape[1]
    tile = min(n, 256)
    left = halves(jnp.concatenate([v_ref[...], x_ref[...]], axis=1))
    for at in range(0, n, tile):
        cut = pl.ds(at, tile)
        o_ref[:, cut] = a_ref[:, cut] - dot3(left, (rh[:, cut], rl[:, cut]))


def finish(matrix, refl, x_rows, rh, rl):
    m, n = matrix.shape
    block = min(m, 512)
    return pl.pallas_call(
        finish_kernel,
        grid=(m // block,),
        out_shape=jax.ShapeDtypeStruct((m, n), F32),
        in_specs=[
            pl.BlockSpec((block, n), lambda g: (g, 0)),
            pl.BlockSpec((block, NB), lambda g: (g, 0)),
            pl.BlockSpec((block, NB), lambda g: (g, 0)),
            pl.BlockSpec((2 * NB, n), lambda g: (0, 0)),
            pl.BlockSpec((2 * NB, n), lambda g: (0, 0)),
        ],
        out_specs=pl.BlockSpec((block, n), lambda g: (g, 0)),
        compiler_params=pltpu.CompilerParams(vmem_limit_bytes=48 * 1024 * 1024),
        cost_estimate=pl.CostEstimate(flops=12 * m * n * NB, bytes_accessed=8 * m * n, transcendentals=0),
        name="finish",
    )(matrix, refl, x_rows, rh, rl)


def body(matrix):
    n_row, n_col = lax.axis_size("row"), lax.axis_size("col")
    refl, x_rows, rh, rl, v_out, w_out = panel(matrix, n_row, n_col)
    updated = finish(matrix, refl, x_rows, rh, rl)
    return updated, v_out[None], w_out[None]


def solution(mesh):
    return jax.shard_map(
        body,
        mesh=mesh,
        in_specs=(P("row", "col"),),
        out_specs=(P("row", "col"), P(None, ("row", "col"), None), P(None, ("row", "col"), None)),
        check_vma=False,
    )
```

```python
import functools

import jax
import jax.numpy as jnp
from jax import lax
from jax.experimental import pallas as pl
from jax.experimental.pallas import tpu as pltpu
from jax.sharding import PartitionSpec as P

NB = 256
STRIP = 16
LANES = 128
MESH = pl.DeviceIdType.MESH
F32 = jnp.float32
BF16 = jnp.bfloat16


def exact(left, right, dims=((1,), (0,))):
    return lax.dot_general(
        left, right, (dims, ((), ())),
        precision=lax.Precision.HIGHEST, preferred_element_type=F32,
    )


def halves(value):
    high = value.astype(BF16)
    return high, (value - high.astype(F32)).astype(BF16)


def dot(left, right, dims=((1,), (0,))):
    return lax.dot_general(left, right, (dims, ((), ())), preferred_element_type=F32)


def dot3(left, right, dims=((1,), (0,))):
    (lh, ll), (rh, rl) = left, right
    return dot(lh, rh, dims) + (dot(lh, rl, dims) + dot(ll, rh, dims))


def wide(part, n):
    return jnp.concatenate([part] * (n // part.shape[1]), axis=1)


FACTOR_SCRATCH = 7


def factor_scratch(n):
    return [pltpu.VMEM((n, n), F32)] * FACTOR_SCRATCH + [pltpu.VMEM((n, LANES), F32)]


def factor_body(gram, top, rinvt_out, linv_out, shape_out, low_out, tft_out,
                wg, wt, fg, ft, lead, bd, bl, sg):
    n = gram.shape[0]
    strip = STRIP
    lanes = lax.broadcasted_iota(jnp.int32, (strip, n), 1)
    subs = lax.broadcasted_iota(jnp.int32, (strip, n), 0)
    lane = lax.broadcasted_iota(jnp.int32, (1, n), 1)
    subs1 = lax.broadcasted_iota(jnp.int32, (strip, LANES), 0)
    full = lax.broadcasted_iota(jnp.int32, (n, n), 1)
    wg[...] = gram
    wt[...] = top
    lead[...] = jnp.zeros_like(lead)

    def one(s, carry):
        at = pl.ds(pl.multiple_of(s * strip, strip), strip)
        g, t = wg[at, :], wt[at, :]
        keep = n - s * strip
        gc = [jnp.broadcast_to(g[:, j : j + 1], (strip, LANES)) for j in range(strip)]
        tc = [jnp.broadcast_to(t[:, j : j + 1], (strip, LANES)) for j in range(strip)]
        gf, tf, ld = g, t, jnp.where(lanes == subs, 1.0, 0.0)
        signs = jnp.zeros((strip, LANES), F32)
        for k in range(strip):
            gcol, gp = gc[k], gc[k][k : k + 1]
            root = 1.0 / jnp.sqrt(gp)
            ginv = root * root
            tcol, tp = tc[k], tc[k][k : k + 1]
            sign = jnp.where(tp >= 0, 1.0, -1.0)
            add = sign * root
            tinv = 1.0 / (tp + add * gp)
            grow = g[k : k + 1]
            trow = t[k : k + 1] + jnp.where((lane >= k) & (lane < keep), grow, 0.0) * wide(add, n)
            gf = jnp.where(subs == k, grow, gf)
            tf = jnp.where(subs == k, trow, tf)
            signs = jnp.where(subs1 == k, sign, signs)
            gscaled = jnp.where(lane == k, wide(ginv, n), grow * wide(ginv, n))
            tscaled = jnp.where(lane == k, wide(tinv, n), trow * wide(tinv, n))
            ld = jnp.where((lanes == k) & (subs > k), wide(tcol * tinv, n), ld)
            for j in range(k + 1, strip):
                grj = gc[j][k : k + 1]
                trj = (tc[j][k : k + 1] + add * grj) * tinv
                grj = grj * ginv
                gc[j] = jnp.where(subs1 == k, grj, gc[j] - gcol * grj)
                tc[j] = jnp.where(subs1 == k, trj, tc[j] - tcol * trj)
            g = jnp.where(subs == k, gscaled, jnp.where(lanes == k, 0.0, g) - wide(gcol, n) * gscaled)
            t = jnp.where(subs == k, tscaled, jnp.where(lanes == k, 0.0, t) - wide(tcol, n) * tscaled)
        back = s * strip
        fg[at, :] = pltpu.roll(gf, back, 1)
        ft[at, :] = pltpu.roll(tf, back, 1)
        bl[at, :] = pltpu.roll(ld, back, 1)
        bd[at, :] = pltpu.roll(jnp.where(lanes < strip, t, 0.0), back, 1)
        sg[at, :] = signs
        gw, tw = wg[...], wt[...]
        step = n - strip
        lead[...] = pltpu.roll(jnp.where(full < strip, tw, lead[...]), step, 1)
        gn = jnp.where(full < strip, 0.0, gw) - exact(gw[:, :strip], g)
        tn = jnp.where(full < strip, 0.0, tw) - exact(tw[:, :strip], t)
        wg[...] = pltpu.roll(gn, step, 1)
        wt[...] = pltpu.roll(tn, step, 1)
        wg[at, :] = pltpu.roll(g, step, 1)
        wt[at, :] = pltpu.roll(t, step, 1)
        return carry

    lax.fori_loop(0, n // strip, one, 0)
    rows = lax.broadcasted_iota(jnp.int32, (n, n), 0)
    cols = lax.broadcasted_iota(jnp.int32, (n, n), 1)
    eye = jnp.where(rows == cols, 1.0, 0.0)
    diag = jnp.sum(fg[...] * eye, axis=1, keepdims=True)
    rinvt = jnp.where(rows > cols, fg[...], eye) * (1.0 / jnp.sqrt(diag)) * wide(sg[...], n)
    linv = jnp.where(rows > cols, ft[...], eye)
    upper = jnp.where(rows <= cols, ft[...], 0.0)
    rinvt_out[...] = rinvt
    linv_out[...] = linv
    tft_out[...] = exact(linv, exact(rinvt, upper, ((1,), (1,))))
    low = exact(exact(jnp.where(rows >= cols - cols % strip, lead[...], 0.0), bd[...]), bl[...])
    low = jnp.where(rows > cols, low, eye)
    low_out[...] = low
    shape_out[...] = jnp.where(rows <= cols, exact(wt[...], low), 0.0)


def greet(partners):
    barrier = pltpu.get_barrier_semaphore()
    for device in partners:
        pl.semaphore_signal(barrier, inc=1, device_id=device, device_id_type=MESH)
    pl.semaphore_wait(barrier, len(partners))


def cross(r, c, n_row, n_col):
    return ([(lax.rem(r + k, n_row), c) for k in range(1, n_row)]
            + [(r, lax.rem(c + k, n_col)) for k in range(1, n_col)])


def trees(x, z, wide_x, deep_z):
    first = [
        ((z == 0) & (x < wide_x - 1), x + 1, z),
        ((x == wide_x - 1) & (z < deep_z - 1), x, z + 1),
        ((z > 0) & (x > 0), x - 1, z),
    ]
    second = [
        ((x == 0) & (z < deep_z - 1), x, z + 1),
        ((z > 0) & (x < wide_x - 1), x + 1, z),
        ((z == 1) & (x > 0), x, z - 1),
    ]
    return first, second


FACTORS = 6
ROWS = 128
DEEP = 256
SKEW = 2


def depths(x, z, wide_x):
    first = jnp.where(z == 0, x, 2 * (wide_x - 1) + z - x)
    second = jnp.where((z == 0) & (x > 0), x + 2, z + x)
    return first, second


def panel_kernel(n_row, n_col, count, extra, a_ref, vr, xr, rh, rl, v_out, w_out,
                 pr, pn, zo, fac, z, ra, rb, abuf, gbuf, xt, vt, inner, cross_sum, isrc, idst, *rest):
    scratch, sems = rest[: FACTOR_SCRATCH + 1], rest[FACTOR_SCRATCH + 1 :]
    (in_sem, a_sem, p_send, p_recv, n_send, n_recv, s_send, s_recv, g_send, g_recv, f_send, f_recv,
     z_send, x_send, x_recv, i_send, i_recv, b_send, b_recv) = sems
    r, c = lax.axis_index("row"), lax.axis_index("col")
    wide_x, deep_z = n_col // n_row, n_row
    x, zz = lax.rem(c, wide_x), c // wide_x
    m, n = a_ref.shape
    rows = ROWS
    half = m // 2
    deep_y = n_row // 2
    y, core = r // 2, lax.rem(r, 2)
    mate = (y * 2 + 1 - core, c)
    greet(cross(r, c, n_row, n_col))

    kids = trees(x, zz, wide_x, deep_z)
    depth = [SKEW * hops for hops in depths(x, zz, wide_x)]
    last_step = SKEW * (2 * wide_x + deep_z - 3)

    def piece(tree, i):
        return pr.at[pl.ds(pl.multiple_of(tree * half + i * rows, rows), rows), :]

    def fact(side, tree, i):
        return fac.at[pl.ds(pl.multiple_of(((side * 2 + tree) * extra + i - count) * rows, rows), rows), :]

    def p_copy(tree, kid, i, there, ref):
        return pltpu.make_async_remote_copy(
            src_ref=ref, dst_ref=ref,
            send_sem=p_send.at[tree, kid, i], recv_sem=p_recv.at[tree, i],
            device_id=(r, there), device_id_type=MESH)

    def forward(tree, i, ref):
        for k, (some, kx, kz) in enumerate(kids[tree]):
            @pl.when(some)
            def _():
                p_copy(tree, k, i, kz * wide_x + kx, ref).start()

    def f_copy(side, tree, i):
        ref = fact(side, tree, i)
        return pltpu.make_async_remote_copy(
            src_ref=ref, dst_ref=ref, send_sem=f_send.at[tree, i - count], recv_sem=f_recv.at[tree, i - count],
            device_id=mate, device_id_type=MESH)

    def deep(tree, i):
        return pl.ds(pl.multiple_of(tree * half + i * DEEP, DEEP), DEEP)

    def a_copies(i, slot):
        return [pltpu.make_async_copy(
            a_ref.at[deep(tree, i), :], abuf.at[slot, pl.ds(tree * DEEP, DEEP), :], a_sem.at[slot, tree])
            for tree in range(2)]

    for copy in a_copies(0, 0):
        copy.start()
    z[...] = jnp.zeros_like(z)
    tile = min(n, 512)

    def multiply(i):
        slot = lax.rem(i, 2)

        @pl.when(i + 1 < half // DEEP)
        def _():
            for copy in a_copies(i + 1, 1 - slot):
                copy.start()
        for copy in a_copies(i, slot):
            copy.wait()
        part = jnp.concatenate([pr[deep(0, i), :], pr[deep(1, i), :]])
        high_low = halves(part.T)
        for at in range(0, n, tile):
            cut = pl.ds(at, tile)
            z[:, cut] += dot3(high_low, halves(abuf[slot, :, cut]))

    def n_copy(kid, there):
        return pltpu.make_async_remote_copy(
            src_ref=pn, dst_ref=pn, send_sem=n_send.at[kid], recv_sem=n_recv.at[0],
            device_id=(there, c), device_id_type=MESH)

    def n_forward():
        @pl.when(y < deep_y - 1)
        def _():
            n_copy(0, r + 2).start()
        n_copy(1, r + 1).start()

    def g_copy(kind, slot, there, sem):
        return pltpu.make_async_remote_copy(
            src_ref=gbuf.at[kind], dst_ref=gbuf.at[slot], send_sem=g_send.at[sem], recv_sem=g_recv.at[sem],
            device_id=(there, c), device_id_type=MESH)

    @pl.when(c == 0)
    def _():
        own = pltpu.make_async_copy(a_ref.at[:, pl.ds(0, NB)], pr, in_sem.at[0])
        own.start()
        own.wait()

        @pl.when(r == 0)
        def _():
            pr[pl.ds(0, NB), :] = jnp.zeros((NB, NB), F32)
            gbuf[1] = pr[pl.ds(NB, NB), :]
            g_copy(1, 1, r + 1, 1).start()

        @pl.loop(0, count)
        def _(i):
            for tree in range(2):
                forward(tree, i, piece(tree, i))

    @pl.when(r == 0)
    def _():
        own = pltpu.make_async_copy(a_ref.at[pl.ds(0, 2 * NB), :], pn, in_sem.at[1])
        own.start()
        own.wait()

        @pl.when(c == 0)
        def _():
            pn[pl.ds(0, NB), pl.ds(0, NB)] = jnp.zeros((NB, NB), F32)

        @pl.when(c != 0)
        def _():
            n_forward()

    @pl.when(c == 0)
    def _():
        gbuf[0] = jnp.zeros((NB, NB), F32)

        @pl.loop(0, m // (4 * NB))
        def _(i):
            part = pr[pl.ds(pl.multiple_of(i * 4 * NB, NB), 4 * NB), :]
            gbuf[0] += exact(part.T, part)

        @pl.when(core == 0)
        def _():
            g_copy(0, 2, r + 1, 0).wait_recv()
            gbuf[0] += gbuf[2]
            for k in range(1, deep_y):
                g_copy(0, 2 + k, lax.rem(y + k, deep_y) * 2, 1 + k).start()
            add = gbuf[0]
            for k in range(1, deep_y):
                g_copy(0, 2 + k, r, 1 + k).wait_recv()
                add = add + gbuf[2 + k]
            gbuf[2 + deep_y] = add
            g_copy(2 + deep_y, 2 + deep_y, r + 1, 0).start()

            @pl.when(y > 0)
            def _():
                g_copy(1, 1, r + 1, 1).wait_recv()

        @pl.when(core == 1)
        def _():
            g_copy(0, 2, r - 1, 0).start()

            @pl.when(y == 0)
            def _():
                g_copy(1, 1, r, 1).wait_recv()
                for k in range(1, deep_y):
                    g_copy(1, 1, k * 2 + 1, 1 + k).start()

            @pl.when(y > 0)
            def _():
                g_copy(1, 1, r, 1 + y).wait_recv()
                g_copy(1, 1, r - 1, 1).start()
            g_copy(2 + deep_y, 2 + deep_y, r, 0).wait_recv()

        @pl.when(r == 0)
        def _():
            n_forward()

        outs = [fac.at[pl.ds(k * NB, NB), :] for k in range(5)]
        fac[pl.ds(5 * NB, NB), :] = jnp.zeros((NB, NB), F32)
        factor_body(gbuf[2 + deep_y], gbuf[1], *outs, *scratch)
        for e in range(extra):
            for tree in range(2):
                forward(tree, count + e, fact(core, tree, count + e))

        @pl.loop(0, half // DEEP)
        def _(i):
            multiply(i)

        @pl.when(core == 0)
        def _():
            for k in range(1, deep_y):
                g_copy(0, 2 + k, r, 1 + k).wait_send()
            g_copy(2 + deep_y, 2 + deep_y, r + 1, 0).wait_send()

        @pl.when(core == 1)
        def _():
            g_copy(0, 2, r - 1, 0).wait_send()

            @pl.when(y == 0)
            def _():
                for k in range(1, deep_y):
                    g_copy(1, 1, k * 2 + 1, 1 + k).wait_send()

        @pl.when((r == 0) | ((y > 0) & (core == 1)))
        def _():
            g_copy(1, 1, r, 1).wait_send()

    @pl.when(c != 0)
    def _():
        late = jnp.maximum(depth[0], depth[1])

        @pl.loop(0, count + last_step)
        def _(t):
            for tree in range(2):
                i = t - depth[tree]

                @pl.when((i >= 0) & (i < count))
                def _():
                    p_copy(tree, 0, i, c, piece(tree, i)).wait_recv()
                    forward(tree, i, piece(tree, i))

            p = t - late

            @pl.when((p >= 0) & (p < count) & (lax.rem(p, 2) == 1))
            def _():
                multiply(p // 2)

    def take_factors(first, last):
        @pl.when(c != 0)
        def _():
            @pl.loop(first, last)
            def _(t):
                for tree in range(2):
                    i = t - depth[tree]

                    @pl.when((i >= 0) & (i < extra))
                    def _():
                        ref = fact(core, tree, count + i)
                        p_copy(tree, 0, count + i, c, ref).wait_recv()
                        forward(tree, count + i, ref)
                        f_copy(core, tree, count + i).start()

    side = n // 2
    cut = NB // deep_y
    mine = pl.multiple_of(core * side, LANES)
    other = pl.multiple_of((1 - core) * side, LANES)
    to_mate = pltpu.make_async_remote_copy(
        src_ref=z.at[:, pl.ds(other, side)], dst_ref=ra, send_sem=s_send.at[0], recv_sem=s_recv.at[0],
        device_id=mate, device_id_type=MESH)
    to_mate.start()

    @pl.when((r != 0) & (core == 0))
    def _():
        n_copy(0, r).wait_recv()
        n_forward()

    to_mate.wait_recv()
    z[:, pl.ds(mine, side)] += ra[...]
    def band(at):
        return pl.ds(pl.multiple_of(at * cut, cut), cut)

    out = []
    for k in range(1, deep_y):
        there = lax.rem(y + k, deep_y)
        copy = pltpu.make_async_remote_copy(
            src_ref=z.at[band(there), pl.ds(mine, side)], dst_ref=rb.at[k - 1],
            send_sem=s_send.at[1 + k], recv_sem=s_recv.at[1 + k],
            device_id=(there * 2 + core, c), device_id_type=MESH)
        copy.start()
        out.append(copy)
    pause = extra + last_step // 2
    take_factors(0, pause)
    added = z[band(y), pl.ds(mine, side)]
    for k in range(1, deep_y):
        out[k - 1].wait_recv()
        added = added + rb[k - 1]
    zo[band(y), pl.ds(mine, side)] = added
    back = []
    for k in range(1, deep_y):
        there = lax.rem(y + k, deep_y)
        came = lax.rem(y - k + deep_y, deep_y)
        pair = [pltpu.make_async_remote_copy(
            src_ref=zo.at[band(where), pl.ds(mine, side)], dst_ref=zo.at[band(where), pl.ds(mine, side)],
            send_sem=s_send.at[1 + deep_y + k], recv_sem=s_recv.at[1 + deep_y + k],
            device_id=(there * 2 + core, c), device_id_type=MESH) for where in (y, came)]
        pair[0].start()
        back.append(pair)
    take_factors(pause, extra + last_step)
    for _, got in back:
        got.wait_recv()
    swap, swap_in = [pltpu.make_async_remote_copy(
        src_ref=zo.at[:, pl.ds(at, side)], dst_ref=zo.at[:, pl.ds(at, side)],
        send_sem=s_send.at[1], recv_sem=s_recv.at[1], device_id=mate, device_id_type=MESH) for at in (mine, other)]
    swap.start()
    swap_in.wait_recv()

    @pl.when(core == 1)
    def _():
        n_copy(1, r).wait_recv()

    @pl.when(c != 0)
    def _():
        for tree in range(2):
            for e in range(extra):
                f_copy(1 - core, tree, count + e).wait_recv()

    rinvt, linv, shape, tft, low = [fac.at[pl.ds(k * NB, NB), :] for k in (0, 1, 2, 4, 3)]

    x_count = n // ROWS
    own_block = pl.multiple_of(x * n, n)

    def x_piece(block, i):
        return xr.at[pl.ds(pl.multiple_of(block * n + i * ROWS, ROWS), ROWS), :]

    def x_copy(block, i, sem, there):
        return pltpu.make_async_remote_copy(
            src_ref=x_piece(block, i), dst_ref=x_piece(block, i), send_sem=sem, recv_sem=x_recv.at[block, i],
            device_id=(r, there), device_id_type=MESH)

    up = (zz >= r) & (zz < n_row - 1)
    down = (zz <= r) & (zz > 0)

    def take_own(i):
        @pl.when(zz != r)
        def _():
            x_copy(x, i, z_send.at[0, i], c).wait_recv()

        @pl.when(up)
        def _():
            x_copy(x, i, z_send.at[0, i], c + wide_x).start()

        @pl.when(down)
        def _():
            x_copy(x, i, z_send.at[1, i], c - wide_x).start()

        @pl.when(x < wide_x - 1)
        def _():
            x_copy(x, i, x_send.at[0, x, i], c + 1).start()

        @pl.when(x > 0)
        def _():
            x_copy(x, i, x_send.at[1, x, i], c - 1).start()

    for at in range(0, n, tile):
        cut_n = pl.ds(at, tile)
        value = exact(linv[...], exact(rinvt[...], zo[:, cut_n]) + pn[pl.ds(NB, NB), cut_n])
        xt[:, cut_n] = value

        @pl.when(zz == r)
        def _():
            xr[pl.ds(pl.multiple_of(own_block + at, tile), tile), :] = value.T
            for i in range(at // ROWS, (at + tile) // ROWS):
                take_own(i)

    shape_parts = halves(shape[...])
    shape_turned = halves(shape[...].T)
    ids = lax.broadcasted_iota(jnp.int32, (NB, NB), 0)
    for at in range(0, n, tile):
        cut_n = pl.ds(at, tile)
        vt[:, cut_n] = dot3(shape_turned, halves(pn[pl.ds(0, NB), cut_n]))

    @pl.when(c == 0)
    def _():
        vt[:, pl.ds(NB, NB)] = low[...].T
    inner[...] = jnp.zeros_like(inner)
    for at in range(0, n, tile):
        cut_n = pl.ds(at, tile)
        inner[...] += exact(vt[:, cut_n], xt[:, cut_n], ((1,), (1,)))

    strip = NB // n_row
    own_strip = pl.ds(pl.multiple_of(r * strip, 8), strip)
    mates = []
    step = 1
    while step < wide_x:
        mates.append(c + step * (1 - 2 * lax.rem(x // step, 2)))
        step *= 2
    step = 1
    while step < deep_z:
        mates.append(c + wide_x * step * (1 - 2 * lax.rem(zz // step, 2)))
        step *= 2
    stages = len(mates)

    def i_copy(k):
        return pltpu.make_async_remote_copy(
            src_ref=isrc.at[k], dst_ref=idst.at[k], send_sem=i_send.at[k], recv_sem=i_recv.at[k],
            device_id=(r, mates[k]), device_id_type=MESH)

    def b_copy(k, receive):
        at = lax.rem(r - k + n_row, n_row) if receive else r
        spot = cross_sum.at[pl.ds(pl.multiple_of(at * strip, 8), strip), :]
        return pltpu.make_async_remote_copy(
            src_ref=spot, dst_ref=spot, send_sem=b_send.at[k - 1], recv_sem=b_recv.at[k - 1],
            device_id=(lax.rem(r + k, n_row), c), device_id_type=MESH)

    isrc[0] = inner[own_strip, :]
    i_copy(0).start()

    @pl.loop(0, m // NB)
    def _(g):
        here = pl.ds(pl.multiple_of(g * NB, NB), NB)
        vr[here, :] = dot3(halves(pr[here, :]), shape_parts)

    @pl.when(r == 0)
    def _():
        vr[pl.ds(NB, NB), :] = low[...]

    depth_z = SKEW * jnp.abs(zz - r)

    @pl.loop(0, max(x_count + SKEW * (deep_z + wide_x - 2), 2 * stages + 4))
    def _(t):
        i_own = t - depth_z

        @pl.when((zz != r) & (i_own >= 0) & (i_own < x_count))
        def _():
            take_own(i_own)

        for block in range(wide_x):
            i = t - depth_z - SKEW * jnp.abs(block - x)

            @pl.when((block != x) & (i >= 0) & (i < x_count))
            def _():
                x_copy(block, i, x_send.at[0, block, i], c).wait_recv()

                @pl.when((block < x) & (x < wide_x - 1))
                def _():
                    x_copy(block, i, x_send.at[0, block, i], c + 1).start()

                @pl.when((block > x) & (x > 0))
                def _():
                    x_copy(block, i, x_send.at[1, block, i], c - 1).start()

        for k in range(stages):
            @pl.when(t == 2 * k + 1)
            def _():
                i_copy(k).wait_recv()
                if k + 1 < stages:
                    isrc[k + 1] = isrc[k] + idst[k]
                    i_copy(k + 1).start()
                else:
                    cross_sum[own_strip, :] = isrc[k] + idst[k]
                    for j in range(1, n_row):
                        b_copy(j, False).start()

        @pl.when(t == 2 * stages + 3)
        def _():
            for j in range(1, n_row):
                b_copy(j, True).wait_recv()
            half_h = 0.5 * exact(tft[...], cross_sum[...])
            gbuf[0] = half_h
            both = halves(half_h + half_h.T)
            for at in range(0, n, tile):
                cut_n = pl.ds(at, tile)
                v_parts = halves(vt[:, cut_n])
                g_parts = halves(xt[:, cut_n] - dot3(both, v_parts))
                rh[pl.ds(0, NB), cut_n], rl[pl.ds(0, NB), cut_n] = g_parts
                rh[pl.ds(NB, NB), cut_n], rl[pl.ds(NB, NB), cut_n] = v_parts

    share = m // n_col
    mine_rows = pl.ds(pl.multiple_of(c * share, 8), share)
    v_mine = vr[mine_rows, :]
    v_out[...] = v_mine
    w_out[...] = xr[mine_rows, :] - exact(v_mine, gbuf[0])

    for k in range(stages):
        i_copy(k).wait_send()
    for j in range(1, n_row):
        b_copy(j, False).wait_send()

    def drain(some, block, sems_of):
        @pl.when(some)
        def _():
            @pl.loop(0, x_count)
            def _(i):
                x_copy(block, i, sems_of(i), c).wait_send()

    drain(up, 0, lambda i: z_send.at[0, i])
    drain(down, 0, lambda i: z_send.at[1, i])
    for block in range(wide_x):
        drain((block <= x) & (x < wide_x - 1), block, lambda i: x_send.at[0, block, i])
        drain((block >= x) & (x > 0), block, lambda i: x_send.at[1, block, i])

    to_mate.wait_send()
    swap.wait_send()
    for copy in out:
        copy.wait_send()
    for sent, _ in back:
        sent.wait_send()

    @pl.when((core == 0) & (y < deep_y - 1))
    def _():
        n_copy(0, r).wait_send()

    @pl.when(core == 0)
    def _():
        n_copy(1, r).wait_send()

    @pl.when(c != 0)
    def _():
        for tree in range(2):
            for e in range(extra):
                f_copy(core, tree, count + e).wait_send()

    for tree in range(2):
        for k, (some, _, _) in enumerate(kids[tree]):
            @pl.when(some)
            def _():
                @pl.loop(0, count)
                def _(i):
                    p_copy(tree, k, i, c, piece(tree, i)).wait_send()
                for e in range(extra):
                    p_copy(tree, k, count + e, c, fact(core, tree, count + e)).wait_send()


def panel(matrix, n_row, n_col):
    m, n = matrix.shape
    count = m // (2 * ROWS)
    extra = FACTORS * NB // (4 * ROWS)
    side = n // 2
    deep_y = n_row // 2
    wide_x = n_col // n_row
    x_count = n // ROWS
    share = m // n_col
    stages = (wide_x.bit_length() - 1) + (n_row.bit_length() - 1)
    dma = pltpu.SemaphoreType.DMA
    vmem = pl.BlockSpec(memory_space=pltpu.VMEM)
    return pl.pallas_call(
        functools.partial(panel_kernel, n_row, n_col, count, extra),
        out_shape=[
            jax.ShapeDtypeStruct((m, NB), F32),
            jax.ShapeDtypeStruct((m, NB), F32),
            jax.ShapeDtypeStruct((2 * NB, n), BF16),
            jax.ShapeDtypeStruct((2 * NB, n), BF16),
            jax.ShapeDtypeStruct((share, NB), F32),
            jax.ShapeDtypeStruct((share, NB), F32),
        ],
        in_specs=[pl.BlockSpec(memory_space=pl.ANY)],
        out_specs=[vmem] * 6,
        scratch_shapes=[
            pltpu.VMEM((m, NB), F32),
            pltpu.VMEM((2 * NB, n), F32),
            pltpu.VMEM((NB, n), F32),
            pltpu.VMEM((FACTORS * NB, NB), F32),
            pltpu.VMEM((NB, n), F32),
            pltpu.VMEM((NB, side), F32),
            pltpu.VMEM((max(deep_y - 1, 1), NB // deep_y, side), F32),
            pltpu.VMEM((2, 2 * DEEP, n), F32),
            pltpu.VMEM((3 + deep_y, NB, NB), F32),
            pltpu.VMEM((NB, n), F32),
            pltpu.VMEM((NB, n), F32),
            pltpu.VMEM((NB, NB), F32),
            pltpu.VMEM((NB, NB), F32),
            pltpu.VMEM((stages, NB // n_row, NB), F32),
            pltpu.VMEM((stages, NB // n_row, NB), F32),
            *factor_scratch(NB),
            dma((2,)), dma((2, 2)),
            dma((2, 3, count + extra)), dma((2, count + extra)),
            dma((2,)), dma((1,)),
            dma((2 + 2 * deep_y,)), dma((2 + 2 * deep_y,)),
            dma((1 + deep_y,)), dma((1 + deep_y,)),
            dma((2, extra)), dma((2, extra)),
            dma((2, x_count)), dma((2, wide_x, x_count)), dma((wide_x, x_count)),
            dma((stages,)), dma((stages,)), dma((n_row - 1,)), dma((n_row - 1,)),
        ],
        compiler_params=pltpu.CompilerParams(
            collective_id=0, has_side_effects=True, vmem_limit_bytes=60 * 1024 * 1024),
        cost_estimate=pl.CostEstimate(flops=6 * m * n * NB, bytes_accessed=4 * m * n, transcendentals=0),
        name="panel",
    )(matrix)


def finish_kernel(a_ref, v_ref, x_ref, rh, rl, o_ref):
    n = a_ref.shape[1]
    tile = min(n, 256)
    left = halves(jnp.concatenate([v_ref[...], x_ref[...]], axis=1))
    for at in range(0, n, tile):
        cut = pl.ds(at, tile)
        o_ref[:, cut] = a_ref[:, cut] - dot3(left, (rh[:, cut], rl[:, cut]))


def finish(matrix, refl, x_rows, rh, rl):
    m, n = matrix.shape
    block = min(m, 512)
    return pl.pallas_call(
        finish_kernel,
        grid=(m // block,),
        out_shape=jax.ShapeDtypeStruct((m, n), F32),
        in_specs=[
            pl.BlockSpec((block, n), lambda g: (g, 0)),
            pl.BlockSpec((block, NB), lambda g: (g, 0)),
            pl.BlockSpec((block, NB), lambda g: (g, 0)),
            pl.BlockSpec((2 * NB, n), lambda g: (0, 0)),
            pl.BlockSpec((2 * NB, n), lambda g: (0, 0)),
        ],
        out_specs=pl.BlockSpec((block, n), lambda g: (g, 0)),
        compiler_params=pltpu.CompilerParams(vmem_limit_bytes=48 * 1024 * 1024),
        cost_estimate=pl.CostEstimate(flops=12 * m * n * NB, bytes_accessed=8 * m * n, transcendentals=0),
        name="finish",
    )(matrix, refl, x_rows, rh, rl)


def body(matrix):
    n_row, n_col = lax.axis_size("row"), lax.axis_size("col")
    refl, x_rows, rh, rl, v_out, w_out = panel(matrix, n_row, n_col)
    updated = finish(matrix, refl, x_rows, rh, rl)
    return updated, v_out[None], w_out[None]


def solution(mesh):
    return jax.shard_map(
        body,
        mesh=mesh,
        in_specs=(P("row", "col"),),
        out_specs=(P("row", "col"), P(None, ("row", "col"), None), P(None, ("row", "col"), None)),
        check_vma=False,
    )
```

```python
import functools

import jax
import jax.numpy as jnp
from jax import lax
from jax.experimental import pallas as pl
from jax.experimental.pallas import tpu as pltpu
from jax.sharding import PartitionSpec as P

NB = 256
STRIP = 16
LANES = 128
MESH = pl.DeviceIdType.MESH
F32 = jnp.float32
BF16 = jnp.bfloat16


def exact(left, right, dims=((1,), (0,))):
    return lax.dot_general(
        left, right, (dims, ((), ())),
        precision=lax.Precision.HIGHEST, preferred_element_type=F32,
    )


def halves(value):
    high = value.astype(BF16)
    return high, (value - high.astype(F32)).astype(BF16)


def dot(left, right, dims=((1,), (0,))):
    return lax.dot_general(left, right, (dims, ((), ())), preferred_element_type=F32)


def dot3(left, right, dims=((1,), (0,))):
    (lh, ll), (rh, rl) = left, right
    return dot(lh, rh, dims) + (dot(lh, rl, dims) + dot(ll, rh, dims))


def wide(part, n):
    return jnp.concatenate([part] * (n // part.shape[1]), axis=1)


FACTOR_SCRATCH = 7


def factor_scratch(n):
    return [pltpu.VMEM((n, n), F32)] * FACTOR_SCRATCH + [pltpu.VMEM((n, LANES), F32)]


def factor_body(gram, top, rinvt_out, linv_out, shape_out, low_out, tft_out,
                wg, wt, fg, ft, lead, bd, bl, sg):
    n = gram.shape[0]
    strip = STRIP
    lanes = lax.broadcasted_iota(jnp.int32, (strip, n), 1)
    subs = lax.broadcasted_iota(jnp.int32, (strip, n), 0)
    lane = lax.broadcasted_iota(jnp.int32, (1, n), 1)
    subs1 = lax.broadcasted_iota(jnp.int32, (strip, LANES), 0)
    full = lax.broadcasted_iota(jnp.int32, (n, n), 1)
    wg[...] = gram
    wt[...] = top
    lead[...] = jnp.zeros_like(lead)

    def one(s, carry):
        at = pl.ds(pl.multiple_of(s * strip, strip), strip)
        g, t = wg[at, :], wt[at, :]
        keep = n - s * strip
        gc = [jnp.broadcast_to(g[:, j : j + 1], (strip, LANES)) for j in range(strip)]
        tc = [jnp.broadcast_to(t[:, j : j + 1], (strip, LANES)) for j in range(strip)]
        gf, tf, ld = g, t, jnp.where(lanes == subs, 1.0, 0.0)
        signs = jnp.zeros((strip, LANES), F32)
        for k in range(strip):
            gcol, gp = gc[k], gc[k][k : k + 1]
            root = 1.0 / jnp.sqrt(gp)
            ginv = root * root
            tcol, tp = tc[k], tc[k][k : k + 1]
            sign = jnp.where(tp >= 0, 1.0, -1.0)
            add = sign * root
            tinv = 1.0 / (tp + add * gp)
            grow = g[k : k + 1]
            trow = t[k : k + 1] + jnp.where((lane >= k) & (lane < keep), grow, 0.0) * wide(add, n)
            gf = jnp.where(subs == k, grow, gf)
            tf = jnp.where(subs == k, trow, tf)
            signs = jnp.where(subs1 == k, sign, signs)
            gscaled = jnp.where(lane == k, wide(ginv, n), grow * wide(ginv, n))
            tscaled = jnp.where(lane == k, wide(tinv, n), trow * wide(tinv, n))
            ld = jnp.where((lanes == k) & (subs > k), wide(tcol * tinv, n), ld)
            for j in range(k + 1, strip):
                grj = gc[j][k : k + 1]
                trj = (tc[j][k : k + 1] + add * grj) * tinv
                grj = grj * ginv
                gc[j] = jnp.where(subs1 == k, grj, gc[j] - gcol * grj)
                tc[j] = jnp.where(subs1 == k, trj, tc[j] - tcol * trj)
            g = jnp.where(subs == k, gscaled, jnp.where(lanes == k, 0.0, g) - wide(gcol, n) * gscaled)
            t = jnp.where(subs == k, tscaled, jnp.where(lanes == k, 0.0, t) - wide(tcol, n) * tscaled)
        back = s * strip
        fg[at, :] = pltpu.roll(gf, back, 1)
        ft[at, :] = pltpu.roll(tf, back, 1)
        bl[at, :] = pltpu.roll(ld, back, 1)
        bd[at, :] = pltpu.roll(jnp.where(lanes < strip, t, 0.0), back, 1)
        sg[at, :] = signs
        gw, tw = wg[...], wt[...]
        step = n - strip
        lead[...] = pltpu.roll(jnp.where(full < strip, tw, lead[...]), step, 1)
        gn = jnp.where(full < strip, 0.0, gw) - exact(gw[:, :strip], g)
        tn = jnp.where(full < strip, 0.0, tw) - exact(tw[:, :strip], t)
        wg[...] = pltpu.roll(gn, step, 1)
        wt[...] = pltpu.roll(tn, step, 1)
        wg[at, :] = pltpu.roll(g, step, 1)
        wt[at, :] = pltpu.roll(t, step, 1)
        return carry

    lax.fori_loop(0, n // strip, one, 0)
    rows = lax.broadcasted_iota(jnp.int32, (n, n), 0)
    cols = lax.broadcasted_iota(jnp.int32, (n, n), 1)
    eye = jnp.where(rows == cols, 1.0, 0.0)
    diag = jnp.sum(fg[...] * eye, axis=1, keepdims=True)
    rinvt = jnp.where(rows > cols, fg[...], eye) * (1.0 / jnp.sqrt(diag)) * wide(sg[...], n)
    linv = jnp.where(rows > cols, ft[...], eye)
    upper = jnp.where(rows <= cols, ft[...], 0.0)
    rinvt_out[...] = rinvt
    linv_out[...] = linv
    tft_out[...] = exact(linv, exact(rinvt, upper, ((1,), (1,))))
    low = exact(exact(jnp.where(rows >= cols - cols % strip, lead[...], 0.0), bd[...]), bl[...])
    low = jnp.where(rows > cols, low, eye)
    low_out[...] = low
    shape_out[...] = jnp.where(rows <= cols, exact(wt[...], low), 0.0)


def greet(partners):
    barrier = pltpu.get_barrier_semaphore()
    for device in partners:
        pl.semaphore_signal(barrier, inc=1, device_id=device, device_id_type=MESH)
    pl.semaphore_wait(barrier, len(partners))


def cross(r, c, n_row, n_col):
    return ([(lax.rem(r + k, n_row), c) for k in range(1, n_row)]
            + [(r, lax.rem(c + k, n_col)) for k in range(1, n_col)])


def trees(x, z, wide_x, deep_z):
    first = [
        ((z == 0) & (x < wide_x - 1), x + 1, z),
        ((x == wide_x - 1) & (z < deep_z - 1), x, z + 1),
        ((z > 0) & (x > 0), x - 1, z),
    ]
    second = [
        ((x == 0) & (z < deep_z - 1), x, z + 1),
        ((z > 0) & (x < wide_x - 1), x + 1, z),
        ((z == 1) & (x > 0), x, z - 1),
    ]
    return first, second


FACTORS = 6
ROWS = 128
DEEP = 256
SKEW = 2


def depths(x, z, wide_x):
    first = jnp.where(z == 0, x, 2 * (wide_x - 1) + z - x)
    second = jnp.where((z == 0) & (x > 0), x + 2, z + x)
    return first, second


def panel_kernel(n_row, n_col, count, extra, a_ref, vr, xr, rh, rl, v_out, w_out,
                 pr, pn, zo, fac, z, ra, rb, abuf, gbuf, xt, vt, inner, cross_sum, isrc, idst, *rest):
    scratch, sems = rest[: FACTOR_SCRATCH + 1], rest[FACTOR_SCRATCH + 1 :]
    (in_sem, a_sem, p_send, p_recv, n_send, n_recv, s_send, s_recv, g_send, g_recv, f_send, f_recv,
     z_send, x_send, x_recv, i_send, i_recv, b_send, b_recv) = sems
    r, c = lax.axis_index("row"), lax.axis_index("col")
    wide_x, deep_z = n_col // n_row, n_row
    x, zz = lax.rem(c, wide_x), c // wide_x
    m, n = a_ref.shape
    rows = ROWS
    half = m // 2
    deep_y = n_row // 2
    y, core = r // 2, lax.rem(r, 2)
    mate = (y * 2 + 1 - core, c)
    greet(cross(r, c, n_row, n_col))

    kids = trees(x, zz, wide_x, deep_z)
    depth = [SKEW * hops for hops in depths(x, zz, wide_x)]
    last_step = SKEW * (2 * wide_x + deep_z - 3)

    def piece(tree, i):
        return pr.at[pl.ds(pl.multiple_of(tree * half + i * rows, rows), rows), :]

    def fact(side, tree, i):
        return fac.at[pl.ds(pl.multiple_of(((side * 2 + tree) * extra + i - count) * rows, rows), rows), :]

    def p_copy(tree, kid, i, there, ref):
        return pltpu.make_async_remote_copy(
            src_ref=ref, dst_ref=ref,
            send_sem=p_send.at[tree, kid, i], recv_sem=p_recv.at[tree, i],
            device_id=(r, there), device_id_type=MESH)

    def forward(tree, i, ref):
        for k, (some, kx, kz) in enumerate(kids[tree]):
            @pl.when(some)
            def _():
                p_copy(tree, k, i, kz * wide_x + kx, ref).start()

    def f_copy(side, tree, i):
        ref = fact(side, tree, i)
        return pltpu.make_async_remote_copy(
            src_ref=ref, dst_ref=ref, send_sem=f_send.at[tree, i - count], recv_sem=f_recv.at[tree, i - count],
            device_id=mate, device_id_type=MESH)

    def deep(tree, i):
        return pl.ds(pl.multiple_of(tree * half + i * DEEP, DEEP), DEEP)

    def a_copies(i, slot):
        return [pltpu.make_async_copy(
            a_ref.at[deep(tree, i), :], abuf.at[slot, pl.ds(tree * DEEP, DEEP), :], a_sem.at[slot, tree])
            for tree in range(2)]

    for copy in a_copies(0, 0):
        copy.start()
    z[...] = jnp.zeros_like(z)
    tile = min(n, 512)

    def multiply(i):
        slot = lax.rem(i, 2)

        @pl.when(i + 1 < half // DEEP)
        def _():
            for copy in a_copies(i + 1, 1 - slot):
                copy.start()
        for copy in a_copies(i, slot):
            copy.wait()
        part = jnp.concatenate([pr[deep(0, i), :], pr[deep(1, i), :]])
        high_low = halves(part.T)
        for at in range(0, n, tile):
            cut = pl.ds(at, tile)
            z[:, cut] += dot3(high_low, halves(abuf[slot, :, cut]))

    def n_copy(kid, there):
        return pltpu.make_async_remote_copy(
            src_ref=pn, dst_ref=pn, send_sem=n_send.at[kid], recv_sem=n_recv.at[0],
            device_id=(there, c), device_id_type=MESH)

    def n_forward():
        @pl.when(y < deep_y - 1)
        def _():
            n_copy(0, r + 2).start()
        n_copy(1, r + 1).start()

    def g_copy(kind, slot, there, sem):
        return pltpu.make_async_remote_copy(
            src_ref=gbuf.at[kind], dst_ref=gbuf.at[slot], send_sem=g_send.at[sem], recv_sem=g_recv.at[sem],
            device_id=(there, c), device_id_type=MESH)

    @pl.when(c == 0)
    def _():
        own = pltpu.make_async_copy(a_ref.at[:, pl.ds(0, NB)], pr, in_sem.at[0])
        own.start()
        own.wait()

        @pl.when(r == 0)
        def _():
            pr[pl.ds(0, NB), :] = jnp.zeros((NB, NB), F32)
            gbuf[1] = pr[pl.ds(NB, NB), :]
            g_copy(1, 1, r + 1, 1).start()

        @pl.loop(0, count)
        def _(i):
            for tree in range(2):
                forward(tree, i, piece(tree, i))

    @pl.when(r == 0)
    def _():
        own = pltpu.make_async_copy(a_ref.at[pl.ds(0, 2 * NB), :], pn, in_sem.at[1])
        own.start()
        own.wait()

        @pl.when(c == 0)
        def _():
            pn[pl.ds(0, NB), pl.ds(0, NB)] = jnp.zeros((NB, NB), F32)

        @pl.when(c != 0)
        def _():
            n_forward()

    @pl.when(c == 0)
    def _():
        gbuf[0] = jnp.zeros((NB, NB), F32)

        @pl.loop(0, m // (4 * NB))
        def _(i):
            part = pr[pl.ds(pl.multiple_of(i * 4 * NB, NB), 4 * NB), :]
            gbuf[0] += exact(part.T, part)

        @pl.when(core == 0)
        def _():
            g_copy(0, 2, r + 1, 0).wait_recv()
            gbuf[0] += gbuf[2]
            for k in range(1, deep_y):
                g_copy(0, 2 + k, lax.rem(y + k, deep_y) * 2, 1 + k).start()
            add = gbuf[0]
            for k in range(1, deep_y):
                g_copy(0, 2 + k, r, 1 + k).wait_recv()
                add = add + gbuf[2 + k]
            gbuf[2 + deep_y] = add
            g_copy(2 + deep_y, 2 + deep_y, r + 1, 0).start()

            @pl.when(y > 0)
            def _():
                g_copy(1, 1, r + 1, 1).wait_recv()

        @pl.when(core == 1)
        def _():
            g_copy(0, 2, r - 1, 0).start()

            @pl.when(y == 0)
            def _():
                g_copy(1, 1, r, 1).wait_recv()
                for k in range(1, deep_y):
                    g_copy(1, 1, k * 2 + 1, 1 + k).start()

            @pl.when(y > 0)
            def _():
                g_copy(1, 1, r, 1 + y).wait_recv()
                g_copy(1, 1, r - 1, 1).start()
            g_copy(2 + deep_y, 2 + deep_y, r, 0).wait_recv()

        @pl.when(r == 0)
        def _():
            n_forward()

        outs = [fac.at[pl.ds(k * NB, NB), :] for k in range(5)]
        fac[pl.ds(5 * NB, NB), :] = jnp.zeros((NB, NB), F32)
        factor_body(gbuf[2 + deep_y], gbuf[1], *outs, *scratch)
        for e in range(extra):
            for tree in range(2):
                forward(tree, count + e, fact(core, tree, count + e))

        @pl.loop(0, half // DEEP)
        def _(i):
            multiply(i)

        @pl.when(core == 0)
        def _():
            for k in range(1, deep_y):
                g_copy(0, 2 + k, r, 1 + k).wait_send()
            g_copy(2 + deep_y, 2 + deep_y, r + 1, 0).wait_send()

        @pl.when(core == 1)
        def _():
            g_copy(0, 2, r - 1, 0).wait_send()

            @pl.when(y == 0)
            def _():
                for k in range(1, deep_y):
                    g_copy(1, 1, k * 2 + 1, 1 + k).wait_send()

        @pl.when((r == 0) | ((y > 0) & (core == 1)))
        def _():
            g_copy(1, 1, r, 1).wait_send()

    @pl.when(c != 0)
    def _():
        late = jnp.maximum(depth[0], depth[1])

        @pl.loop(0, count + last_step)
        def _(t):
            for tree in range(2):
                i = t - depth[tree]

                @pl.when((i >= 0) & (i < count))
                def _():
                    p_copy(tree, 0, i, c, piece(tree, i)).wait_recv()
                    forward(tree, i, piece(tree, i))

            p = t - late

            @pl.when((p >= 0) & (p < count) & (lax.rem(p, 2) == 1))
            def _():
                multiply(p // 2)

    def take_factors(first, last):
        @pl.when(c != 0)
        def _():
            @pl.loop(first, last)
            def _(t):
                for tree in range(2):
                    i = t - depth[tree]

                    @pl.when((i >= 0) & (i < extra))
                    def _():
                        ref = fact(core, tree, count + i)
                        p_copy(tree, 0, count + i, c, ref).wait_recv()
                        forward(tree, count + i, ref)
                        f_copy(core, tree, count + i).start()

    side = n // 2
    cut = NB // deep_y
    mine = pl.multiple_of(core * side, LANES)
    other = pl.multiple_of((1 - core) * side, LANES)
    to_mate = pltpu.make_async_remote_copy(
        src_ref=z.at[:, pl.ds(other, side)], dst_ref=ra, send_sem=s_send.at[0], recv_sem=s_recv.at[0],
        device_id=mate, device_id_type=MESH)
    to_mate.start()

    @pl.when((r != 0) & (core == 0))
    def _():
        n_copy(0, r).wait_recv()
        n_forward()

    to_mate.wait_recv()
    z[:, pl.ds(mine, side)] += ra[...]
    def band(at):
        return pl.ds(pl.multiple_of(at * cut, cut), cut)

    out = []
    for k in range(1, deep_y):
        there = lax.rem(y + k, deep_y)
        copy = pltpu.make_async_remote_copy(
            src_ref=z.at[band(there), pl.ds(mine, side)], dst_ref=rb.at[k - 1],
            send_sem=s_send.at[1 + k], recv_sem=s_recv.at[1 + k],
            device_id=(there * 2 + core, c), device_id_type=MESH)
        copy.start()
        out.append(copy)
    pause = extra + last_step // 2
    take_factors(0, pause)
    added = z[band(y), pl.ds(mine, side)]
    for k in range(1, deep_y):
        out[k - 1].wait_recv()
        added = added + rb[k - 1]
    zo[band(y), pl.ds(mine, side)] = added
    back = []
    for k in range(1, deep_y):
        there = lax.rem(y + k, deep_y)
        came = lax.rem(y - k + deep_y, deep_y)
        pair = [pltpu.make_async_remote_copy(
            src_ref=zo.at[band(where), pl.ds(mine, side)], dst_ref=zo.at[band(where), pl.ds(mine, side)],
            send_sem=s_send.at[1 + deep_y + k], recv_sem=s_recv.at[1 + deep_y + k],
            device_id=(there * 2 + core, c), device_id_type=MESH) for where in (y, came)]
        pair[0].start()
        back.append(pair)
    take_factors(pause, extra + last_step)
    for _, got in back:
        got.wait_recv()
    swap, swap_in = [pltpu.make_async_remote_copy(
        src_ref=zo.at[:, pl.ds(at, side)], dst_ref=zo.at[:, pl.ds(at, side)],
        send_sem=s_send.at[1], recv_sem=s_recv.at[1], device_id=mate, device_id_type=MESH) for at in (mine, other)]
    swap.start()
    swap_in.wait_recv()

    @pl.when(core == 1)
    def _():
        n_copy(1, r).wait_recv()

    @pl.when(c != 0)
    def _():
        for tree in range(2):
            for e in range(extra):
                f_copy(1 - core, tree, count + e).wait_recv()

    rinvt, linv, shape, tft, low = [fac.at[pl.ds(k * NB, NB), :] for k in (0, 1, 2, 4, 3)]

    x_count = n // ROWS
    own_block = pl.multiple_of(x * n, n)

    def x_piece(block, i):
        return xr.at[pl.ds(pl.multiple_of(block * n + i * ROWS, ROWS), ROWS), :]

    def x_copy(block, i, sem, there):
        return pltpu.make_async_remote_copy(
            src_ref=x_piece(block, i), dst_ref=x_piece(block, i), send_sem=sem, recv_sem=x_recv.at[block, i],
            device_id=(r, there), device_id_type=MESH)

    up = (zz >= r) & (zz < n_row - 1)
    down = (zz <= r) & (zz > 0)

    def take_own(i):
        @pl.when(zz != r)
        def _():
            x_copy(x, i, z_send.at[0, i], c).wait_recv()

        @pl.when(up)
        def _():
            x_copy(x, i, z_send.at[0, i], c + wide_x).start()

        @pl.when(down)
        def _():
            x_copy(x, i, z_send.at[1, i], c - wide_x).start()

        @pl.when(x < wide_x - 1)
        def _():
            x_copy(x, i, x_send.at[0, x, i], c + 1).start()

        @pl.when(x > 0)
        def _():
            x_copy(x, i, x_send.at[1, x, i], c - 1).start()

    def x_tile(at):
        cut_n = pl.ds(at, tile)
        value = exact(linv[...], exact(rinvt[...], zo[:, cut_n]) + pn[pl.ds(NB, NB), cut_n])
        xt[:, cut_n] = value
        return value

    @pl.when(zz == r)
    def _():
        for at in range(0, n, tile):
            xr[pl.ds(pl.multiple_of(own_block + at, tile), tile), :] = x_tile(at).T
            for i in range(at // ROWS, (at + tile) // ROWS):
                take_own(i)

    shape_parts = halves(shape[...])
    shape_turned = halves(shape[...].T)
    inner[...] = jnp.zeros_like(inner)
    tiles = n // tile

    def v_tile(at):
        cut_n = pl.ds(at, tile)
        vt[:, cut_n] = dot3(shape_turned, halves(pn[pl.ds(0, NB), cut_n]))
        if at == 0:
            @pl.when(c == 0)
            def _():
                vt[:, pl.ds(NB, NB)] = low[...].T
        inner[...] += exact(vt[:, cut_n], xt[:, cut_n], ((1,), (1,)))

    strip = NB // n_row
    own_strip = pl.ds(pl.multiple_of(r * strip, 8), strip)
    mates = []
    step = 1
    while step < wide_x:
        mates.append(c + step * (1 - 2 * lax.rem(x // step, 2)))
        step *= 2
    step = 1
    while step < deep_z:
        mates.append(c + wide_x * step * (1 - 2 * lax.rem(zz // step, 2)))
        step *= 2
    stages = len(mates)

    def i_copy(k):
        return pltpu.make_async_remote_copy(
            src_ref=isrc.at[k], dst_ref=idst.at[k], send_sem=i_send.at[k], recv_sem=i_recv.at[k],
            device_id=(r, mates[k]), device_id_type=MESH)

    def b_copy(k, receive):
        at = lax.rem(r - k + n_row, n_row) if receive else r
        spot = cross_sum.at[pl.ds(pl.multiple_of(at * strip, 8), strip), :]
        return pltpu.make_async_remote_copy(
            src_ref=spot, dst_ref=spot, send_sem=b_send.at[k - 1], recv_sem=b_recv.at[k - 1],
            device_id=(lax.rem(r + k, n_row), c), device_id_type=MESH)

    depth_z = SKEW * jnp.abs(zz - r)

    @pl.loop(0, max(x_count + SKEW * (deep_z + wide_x - 2), tiles + 2 * stages + 4, m // NB))
    def _(t):
        i_own = t - depth_z

        @pl.when((zz != r) & (i_own >= 0) & (i_own < x_count))
        def _():
            take_own(i_own)

        for block in range(wide_x):
            i = t - depth_z - SKEW * jnp.abs(block - x)

            @pl.when((block != x) & (i >= 0) & (i < x_count))
            def _():
                x_copy(block, i, x_send.at[0, block, i], c).wait_recv()

                @pl.when((block < x) & (x < wide_x - 1))
                def _():
                    x_copy(block, i, x_send.at[0, block, i], c + 1).start()

                @pl.when((block > x) & (x > 0))
                def _():
                    x_copy(block, i, x_send.at[1, block, i], c - 1).start()

        for k in range(tiles):
            @pl.when(t == k)
            def _():
                @pl.when(zz != r)
                def _():
                    x_tile(k * tile)
                v_tile(k * tile)
                if k == tiles - 1:
                    isrc[0] = inner[own_strip, :]
                    i_copy(0).start()

        @pl.when(t < m // NB)
        def _():
            here = pl.ds(pl.multiple_of(t * NB, NB), NB)
            vr[here, :] = dot3(halves(pr[here, :]), shape_parts)

        for k in range(stages):
            @pl.when(t == tiles + 2 * k + 1)
            def _():
                i_copy(k).wait_recv()
                if k + 1 < stages:
                    isrc[k + 1] = isrc[k] + idst[k]
                    i_copy(k + 1).start()
                else:
                    cross_sum[own_strip, :] = isrc[k] + idst[k]
                    for j in range(1, n_row):
                        b_copy(j, False).start()

        @pl.when(t == tiles + 2 * stages + 3)
        def _():
            for j in range(1, n_row):
                b_copy(j, True).wait_recv()
            half_h = 0.5 * exact(tft[...], cross_sum[...])
            gbuf[0] = half_h
            both = halves(half_h + half_h.T)
            for at in range(0, n, tile):
                cut_n = pl.ds(at, tile)
                v_parts = halves(vt[:, cut_n])
                g_parts = halves(xt[:, cut_n] - dot3(both, v_parts))
                rh[pl.ds(0, NB), cut_n], rl[pl.ds(0, NB), cut_n] = g_parts
                rh[pl.ds(NB, NB), cut_n], rl[pl.ds(NB, NB), cut_n] = v_parts

    @pl.when(r == 0)
    def _():
        vr[pl.ds(NB, NB), :] = low[...]

    share = m // n_col
    mine_rows = pl.ds(pl.multiple_of(c * share, 8), share)
    v_mine = vr[mine_rows, :]
    v_out[...] = v_mine
    w_out[...] = xr[mine_rows, :] - exact(v_mine, gbuf[0])

    for k in range(stages):
        i_copy(k).wait_send()
    for j in range(1, n_row):
        b_copy(j, False).wait_send()

    def drain(some, block, sems_of):
        @pl.when(some)
        def _():
            @pl.loop(0, x_count)
            def _(i):
                x_copy(block, i, sems_of(i), c).wait_send()

    drain(up, 0, lambda i: z_send.at[0, i])
    drain(down, 0, lambda i: z_send.at[1, i])
    for block in range(wide_x):
        drain((block <= x) & (x < wide_x - 1), block, lambda i: x_send.at[0, block, i])
        drain((block >= x) & (x > 0), block, lambda i: x_send.at[1, block, i])

    to_mate.wait_send()
    swap.wait_send()
    for copy in out:
        copy.wait_send()
    for sent, _ in back:
        sent.wait_send()

    @pl.when((core == 0) & (y < deep_y - 1))
    def _():
        n_copy(0, r).wait_send()

    @pl.when(core == 0)
    def _():
        n_copy(1, r).wait_send()

    @pl.when(c != 0)
    def _():
        for tree in range(2):
            for e in range(extra):
                f_copy(core, tree, count + e).wait_send()

    for tree in range(2):
        for k, (some, _, _) in enumerate(kids[tree]):
            @pl.when(some)
            def _():
                @pl.loop(0, count)
                def _(i):
                    p_copy(tree, k, i, c, piece(tree, i)).wait_send()
                for e in range(extra):
                    p_copy(tree, k, count + e, c, fact(core, tree, count + e)).wait_send()


def panel(matrix, n_row, n_col):
    m, n = matrix.shape
    count = m // (2 * ROWS)
    extra = FACTORS * NB // (4 * ROWS)
    side = n // 2
    deep_y = n_row // 2
    wide_x = n_col // n_row
    x_count = n // ROWS
    share = m // n_col
    stages = (wide_x.bit_length() - 1) + (n_row.bit_length() - 1)
    dma = pltpu.SemaphoreType.DMA
    vmem = pl.BlockSpec(memory_space=pltpu.VMEM)
    return pl.pallas_call(
        functools.partial(panel_kernel, n_row, n_col, count, extra),
        out_shape=[
            jax.ShapeDtypeStruct((m, NB), F32),
            jax.ShapeDtypeStruct((m, NB), F32),
            jax.ShapeDtypeStruct((2 * NB, n), BF16),
            jax.ShapeDtypeStruct((2 * NB, n), BF16),
            jax.ShapeDtypeStruct((share, NB), F32),
            jax.ShapeDtypeStruct((share, NB), F32),
        ],
        in_specs=[pl.BlockSpec(memory_space=pl.ANY)],
        out_specs=[vmem] * 6,
        scratch_shapes=[
            pltpu.VMEM((m, NB), F32),
            pltpu.VMEM((2 * NB, n), F32),
            pltpu.VMEM((NB, n), F32),
            pltpu.VMEM((FACTORS * NB, NB), F32),
            pltpu.VMEM((NB, n), F32),
            pltpu.VMEM((NB, side), F32),
            pltpu.VMEM((max(deep_y - 1, 1), NB // deep_y, side), F32),
            pltpu.VMEM((2, 2 * DEEP, n), F32),
            pltpu.VMEM((3 + deep_y, NB, NB), F32),
            pltpu.VMEM((NB, n), F32),
            pltpu.VMEM((NB, n), F32),
            pltpu.VMEM((NB, NB), F32),
            pltpu.VMEM((NB, NB), F32),
            pltpu.VMEM((stages, NB // n_row, NB), F32),
            pltpu.VMEM((stages, NB // n_row, NB), F32),
            *factor_scratch(NB),
            dma((2,)), dma((2, 2)),
            dma((2, 3, count + extra)), dma((2, count + extra)),
            dma((2,)), dma((1,)),
            dma((2 + 2 * deep_y,)), dma((2 + 2 * deep_y,)),
            dma((1 + deep_y,)), dma((1 + deep_y,)),
            dma((2, extra)), dma((2, extra)),
            dma((2, x_count)), dma((2, wide_x, x_count)), dma((wide_x, x_count)),
            dma((stages,)), dma((stages,)), dma((n_row - 1,)), dma((n_row - 1,)),
        ],
        compiler_params=pltpu.CompilerParams(
            collective_id=0, has_side_effects=True, vmem_limit_bytes=60 * 1024 * 1024),
        cost_estimate=pl.CostEstimate(flops=6 * m * n * NB, bytes_accessed=4 * m * n, transcendentals=0),
        name="panel",
    )(matrix)


def finish_kernel(a_ref, v_ref, x_ref, rh, rl, o_ref):
    n = a_ref.shape[1]
    tile = min(n, 256)
    left = halves(jnp.concatenate([v_ref[...], x_ref[...]], axis=1))
    for at in range(0, n, tile):
        cut = pl.ds(at, tile)
        o_ref[:, cut] = a_ref[:, cut] - dot3(left, (rh[:, cut], rl[:, cut]))


def finish(matrix, refl, x_rows, rh, rl):
    m, n = matrix.shape
    block = min(m, 512)
    return pl.pallas_call(
        finish_kernel,
        grid=(m // block,),
        out_shape=jax.ShapeDtypeStruct((m, n), F32),
        in_specs=[
            pl.BlockSpec((block, n), lambda g: (g, 0)),
            pl.BlockSpec((block, NB), lambda g: (g, 0)),
            pl.BlockSpec((block, NB), lambda g: (g, 0)),
            pl.BlockSpec((2 * NB, n), lambda g: (0, 0)),
            pl.BlockSpec((2 * NB, n), lambda g: (0, 0)),
        ],
        out_specs=pl.BlockSpec((block, n), lambda g: (g, 0)),
        compiler_params=pltpu.CompilerParams(vmem_limit_bytes=48 * 1024 * 1024),
        cost_estimate=pl.CostEstimate(flops=12 * m * n * NB, bytes_accessed=8 * m * n, transcendentals=0),
        name="finish",
    )(matrix, refl, x_rows, rh, rl)


def body(matrix):
    n_row, n_col = lax.axis_size("row"), lax.axis_size("col")
    refl, x_rows, rh, rl, v_out, w_out = panel(matrix, n_row, n_col)
    updated = finish(matrix, refl, x_rows, rh, rl)
    return updated, v_out[None], w_out[None]


def solution(mesh):
    return jax.shard_map(
        body,
        mesh=mesh,
        in_specs=(P("row", "col"),),
        out_specs=(P("row", "col"), P(None, ("row", "col"), None), P(None, ("row", "col"), None)),
        check_vma=False,
    )
```
